32 devices in a mesh: fsdp: 8 (over y, x, core), dp: 4 (over z).
Axes of the slice: x: 2, y: 2, z: 4, core: 2. Of those that a mesh axis runs over, the one named last changes fastest.
Arguments:
- tokens: bfloat16 [4096, 1024], P(('fsdp', 'dp')), may hold values from -6 to 6
- segment_ids: int32 [4096], P(('fsdp', 'dp')), may hold values from 0 to 4095, as said below
- cotangent: bfloat16 [4096, 1024], P(('fsdp', 'dp')), may hold values from -6 to 6
- w_in: bfloat16 [1024, 3352], P('fsdp'), may hold values from -0.1875 to 0.1875
- w_q: bfloat16 [1024, 512], P('fsdp'), may hold values from -0.5 to 0.5
- w_k: bfloat16 [1024, 128], P('fsdp'), may hold values from -0.5 to 0.5
- w_v: bfloat16 [1024, 128], P('fsdp'), may hold values from -0.1875 to 0.1875
- w_o: bfloat16 [1024, 512], P('fsdp'), may hold values from -0.5 to 0.5
- w_out: bfloat16 [1024, 1536], P('fsdp'), may hold values from -0.15625 to 0.15625
- w_gate: bfloat16 [1024, 2048], P('fsdp'), may hold values from -0.1875 to 0.1875
- w_up: bfloat16 [1024, 2048], P('fsdp'), may hold values from -0.1875 to 0.1875
- w_down: bfloat16 [1024, 2048], P('fsdp'), may hold values from -0.125 to 0.125
- g_in: float32 [1024], replicated, may hold values from 0.5 to 1.5
- g_ff: float32 [1024], replicated, may hold values from 0.5 to 1.5
- g_mamba: float32 [1536], replicated, may hold values from 0.5 to 1.5
- conv_weight: float32 [4, 1792], replicated, may hold values from -3 to 3
- conv_bias: float32 [1792], replicated, may hold values from -3 to 3
- a_log: float32 [24], replicated, may hold values from 0 to 2.8
- d_skip: float32 [24], replicated, may hold values from 0.5 to 1.5
- dt_bias: float32 [24], replicated, may hold values from -5 to -1
Outputs:
- output: bfloat16 [4096, 1024], P(('fsdp', 'dp'))
- grad_tokens: bfloat16 [4096, 1024], P(('fsdp', 'dp'))
- grad_w_in: float32 [1024, 3352], P('fsdp')
- grad_w_q: float32 [1024, 512], P('fsdp')
- grad_w_k: float32 [1024, 128], P('fsdp')
- grad_w_v: float32 [1024, 128], P('fsdp')
- grad_w_o: float32 [1024, 512], P('fsdp')
- grad_w_out: float32 [1024, 1536], P('fsdp')
- grad_w_gate: float32 [1024, 2048], P('fsdp')
- grad_w_up: float32 [1024, 2048], P('fsdp')
- grad_w_down: float32 [1024, 2048], P('fsdp')
- grad_g_in: float32 [1024], replicated
- grad_g_ff: float32 [1024], replicated
- grad_g_mamba: float32 [1536], replicated
- grad_conv_weight: float32 [4, 1792], replicated
- grad_conv_bias: float32 [1792], replicated
- grad_a_log: float32 [24], replicated
- grad_d_skip: float32 [24], replicated
- grad_dt_bias: float32 [24], replicated
The draws below stay inside these ranges and needn't reach their ends.
Inputs may be any that keep to these rules, and one draw needn't show every extreme that they name: `segment_ids`: each id is the row of its sequence's first token in the whole array. Within each device's 128 rows the ids do not decrease and the first row starts a sequence, so no sequence crosses the boundary between two devices' rows; the last token of the whole array is a sequence of its own.
All inputs are finite; a program needn't handle non-finite values.
Results may differ from the reference program's by a relative error of at most 0.013.
Values may be sent and summed in bfloat16 or wider, within the bound.
No kernel may reach another device: no remote copies, remote signals or barrier semaphores. Data moves between devices by JAX's collectives and lax.ppermute only.
A program may use at most 256 MiB of HBM per device.

```python
import jax
import jax.numpy as jnp
from jax import lax

D = 1024
FF = 2048
MH = 24
HD = 64
KC = 4
AH = 8
KVH = 2
TOK_DEV = 128
E = 1536
CONV_CH = 1792
IN_COLS = 3352
Q_COLS = 512
KV_COLS = 128
TOKENS = 4096
N_FSDP = 8
N_DP = 4


def draw_segment_ids(key, part):
    blocks = TOKENS // TOK_DEV
    flags = jax.random.randint(key, (blocks, TOK_DEV), 0, max(TOK_DEV // 3, 2)) == 0
    index_col = jnp.arange(TOK_DEV, dtype=jnp.int32)[None, :]
    block_row = jnp.arange(blocks, dtype=jnp.int32)[:, None]
    flags = flags | (index_col == 0) | (block_row == blocks - 1) & (index_col == TOK_DEV - 1)
    starts = lax.cummax(jnp.where(flags, index_col, 0), axis=1)
    offsets = (jnp.arange(blocks, dtype=jnp.int32) * TOK_DEV)[:, None]
    return (starts + offsets).reshape(TOKENS).astype(jnp.int32)


def weight_base(key, salt_value, columns):
    normal_part = jax.random.normal(jax.random.fold_in(key, salt_value), (D, columns), jnp.float32)
    return jnp.clip(normal_part, -4.0, 4.0) * D ** (-0.5)


def draw_tokens(key, part):
    values = jax.random.normal(jax.random.fold_in(key, 9102), (TOKENS, D), jnp.float32)
    return jnp.clip(values, -6.0, 6.0).astype(jnp.bfloat16)


def draw_w_q(key, part):
    matrix = weight_base(key, 9111, Q_COLS)
    return jnp.clip(matrix, -0.5, 0.5).astype(jnp.bfloat16)


def draw_w_k(key, part):
    matrix = weight_base(key, 9112, KV_COLS)
    return jnp.clip(matrix, -0.5, 0.5).astype(jnp.bfloat16)


def block_levels(rng, dims, cuts, low, top_value):
    def one(dim, blocks):
        heights = jax.random.uniform(jax.random.fold_in(jax.random.fold_in(rng, 6), dim), (blocks,), jnp.float32, low / len(cuts), top_value / len(cuts))
        return jnp.repeat(jnp.exp(heights), dims[dim] // blocks).reshape((-1,) + (1,) * (len(dims) - dim - 1))

    level = one(*cuts[0])
    for cut in cuts[1:]:
        level = level * one(*cut)
    return level


def bell_draw(rng, shape, spread, limit, cuts=(), kind=jnp.bfloat16):
    values = spread * jax.random.normal(rng, shape, jnp.float32)
    if cuts:
        values = values * block_levels(rng, shape, cuts, -0.22, 0.18)
    return jnp.clip(values, -limit, limit).astype(kind)


def setup_inputs(seed: int = 0) -> dict:
    splits = jax.random.split(jax.random.key(seed), 21)
    return {
        "tokens": draw_tokens(jax.random.fold_in(splits[20], 71), 0),
        "segment_ids": draw_segment_ids(jax.random.fold_in(splits[20], 71), 0),
        "cotangent": bell_draw(splits[2], (TOKENS, D), 1.0, 6.0, ((0, 32),)),
        "w_in": bell_draw(splits[3], (D, IN_COLS), D ** -0.5, 0.1875, ((0, 8),)),
        "w_q": draw_w_q(jax.random.fold_in(splits[20], 71), 0),
        "w_k": draw_w_k(jax.random.fold_in(splits[20], 71), 0),
        "w_v": bell_draw(splits[6], (D, KV_COLS), D ** -0.5, 0.1875, ((0, 8),)),
        "w_o": bell_draw(splits[7], (D, Q_COLS), (Q_COLS // 4) ** -0.5, 0.5, ((0, 8),)),
        "w_out": bell_draw(splits[8], (D, E), E ** -0.5, 0.15625, ((0, 8),)),
        "w_gate": bell_draw(splits[9], (D, FF), D ** -0.5, 0.1875, ((0, 8),)),
        "w_up": bell_draw(splits[10], (D, FF), D ** -0.5, 0.1875, ((0, 8),)),
        "w_down": bell_draw(splits[11], (D, FF), FF ** -0.5, 0.125, ((0, 8),)),
        "g_in": jnp.clip(1.0 + 0.1 * jax.random.normal(splits[12], (D,), jnp.float32), 0.5, 1.5),
        "g_ff": jnp.clip(1.0 + 0.1 * jax.random.normal(splits[13], (D,), jnp.float32), 0.5, 1.5),
        "g_mamba": jnp.clip(1.0 + 0.1 * jax.random.normal(splits[14], (E,), jnp.float32), 0.5, 1.5),
        "conv_weight": bell_draw(splits[15], (KC, CONV_CH), KC ** -0.5, 3.0, (), jnp.float32),
        "conv_bias": bell_draw(splits[16], (CONV_CH,), 0.5, 3.0, (), jnp.float32),
        "a_log": jnp.clip(jax.random.uniform(splits[17], (MH,), jnp.float32, 0.0, 2.8), 0.0, 2.8),
        "d_skip": jnp.clip(jax.random.uniform(splits[18], (MH,), jnp.float32, 0.5, 1.5), 0.5, 1.5),
        "dt_bias": jnp.clip(jax.random.uniform(splits[19], (MH,), jnp.float32, -5.0, -1.0), -5.0, -1.0),
    }


norm_eps = 1e-05
rope_base = 10000.0
HIGH = lax.Precision.HIGHEST

def rms_norm(values, gain):
    return values * lax.rsqrt(lax.optimization_barrier(jnp.mean(values * values, -1, keepdims=True)) + norm_eps) * gain

def linked_mask(segment_ids):
    count = segment_ids.shape[0]
    row_ids = jnp.arange(count, dtype=jnp.int32)
    return (row_ids[None, :] <= row_ids[:, None]) & (segment_ids[:, None] == segment_ids[None, :])

def seq_position(segment_ids):
    count = segment_ids.shape[0]
    row_ids = jnp.arange(count, dtype=jnp.int32)
    change = jnp.concatenate([jnp.ones((1,), bool), segment_ids[1:] != segment_ids[:-1]])
    starts = lax.cummax(jnp.where(change, row_ids, 0), axis=0)
    return row_ids - starts

def mamba_mix(projected, conv_weight, conv_bias, a_log, d_skip, dt_bias, norm_gain, segment_ids):
    count = projected.shape[0]
    inner_dim = norm_gain.shape[0]
    channels = conv_bias.shape[0]
    state_dim = (channels - inner_dim) // 2
    heads_count = a_log.shape[0]
    head_dim = inner_dim // heads_count
    kernel = conv_weight.shape[0]
    z_part = projected[:, :inner_dim]
    conv_in = projected[:, inner_dim:inner_dim + channels]
    dt_raw = projected[:, inner_dim + channels:]
    conv_out = conv_in * conv_weight[kernel - 1]
    for offset_lag in range(1, kernel):
        shifted = jnp.concatenate([jnp.zeros((offset_lag, channels), jnp.float32), conv_in[:-offset_lag]], 0)
        seg_shift = jnp.concatenate([jnp.full((offset_lag,), -1, jnp.int32), segment_ids[:-offset_lag]])
        keep_mask = (seg_shift == segment_ids)[:, None]
        conv_out = conv_out + jnp.where(keep_mask, shifted, 0.0) * conv_weight[kernel - 1 - offset_lag]
    act_conv = jax.nn.silu(conv_out + conv_bias)
    x_heads = act_conv[:, :inner_dim].reshape(count, heads_count, head_dim)
    b_mat = act_conv[:, inner_dim:inner_dim + state_dim]
    c_mat = act_conv[:, inner_dim + state_dim:]
    delta_t = jax.nn.softplus(dt_raw + dt_bias)
    log_decay = -delta_t * jnp.exp(a_log)
    cumulative = jnp.cumsum(log_decay, 0).T
    log_gap = cumulative[:, :, None] - cumulative[:, None, :]
    allowed = linked_mask(segment_ids)[None, :, :]
    decay_w = jnp.where(allowed, jnp.exp(jnp.where(allowed, log_gap, 0.0)), 0.0)
    scores = jnp.dot(c_mat, b_mat.T, precision=HIGH)
    mixer_map = scores[None, :, :] * decay_w * delta_t.T[:, None, :]
    y_heads = jnp.einsum('hts,shd->thd', mixer_map, x_heads, precision=HIGH) + d_skip[None, :, None] * x_heads
    gated_out = y_heads.reshape(count, inner_dim) * jax.nn.silu(z_part)
    return rms_norm(gated_out, norm_gain)

def rotate(heads_arr, position):
    half_dim = HD // 2
    frequency = rope_base ** (-jnp.arange(half_dim, dtype=jnp.float32) * 2.0 / HD)
    angles = position.astype(jnp.float32)[:, None] * frequency[None, :]
    cosine = jnp.cos(angles)[:, None, :]
    sine_part = jnp.sin(angles)[:, None, :]
    first = heads_arr[..., :half_dim]
    second = heads_arr[..., half_dim:]
    return jnp.concatenate([first * cosine - second * sine_part, first * sine_part + second * cosine], -1)

def attend(q_all, k_all, v_all, segment_ids):
    count = q_all.shape[0]
    position = seq_position(segment_ids)
    q_rot = rotate(q_all.reshape(count, AH, HD), position).reshape(count, KVH, AH // KVH, HD)
    k_rot = rotate(k_all.reshape(count, KVH, HD), position)
    v_heads = v_all.reshape(count, KVH, HD)
    logits = jnp.einsum('tkgd,skd->kgts', q_rot, k_rot, precision=HIGH) * HD ** (-0.5)
    allowed = linked_mask(segment_ids)[None, None, :, :]
    logits = jnp.where(allowed, logits, -1e+30)
    top_val = lax.optimization_barrier(jnp.max(logits, -1, keepdims=True))
    expo = jnp.exp(logits - top_val)
    probs = expo / lax.optimization_barrier(jnp.sum(expo, -1, keepdims=True))
    return jnp.einsum('kgts,skd->tkgd', probs, v_heads, precision=HIGH).reshape(count, AH * HD)

def mul_t(left, right):
    return lax.dot_general(left, right, (((1,), (1,)), ((), ())), preferred_element_type=jnp.float32)

def t_mul(left, right):
    return lax.dot_general(left, right, (((0,), (0,)), ((), ())), preferred_element_type=jnp.float32)

def swiglu(gate_in, up_in):
    return jax.nn.silu(gate_in) * up_in

def layer_pass(block_tok, block_seg, block_cot, big, small):
    w_in, w_q, w_k, w_v, w_o, w_out, w_gate, w_up, w_down = big
    g_in, g_ff, g_mamba, conv_weight, conv_bias, a_log, d_skip, dt_bias = small
    tok32 = block_tok.astype(jnp.float32)
    normed32, pull_norm_in = jax.vjp(rms_norm, tok32, g_in)
    normed = normed32.astype(jnp.bfloat16)
    projected = jnp.dot(normed, w_in, preferred_element_type=jnp.float32)
    queries = jnp.dot(normed, w_q, preferred_element_type=jnp.float32)
    keys_all = jnp.dot(normed, w_k, preferred_element_type=jnp.float32)
    values_all = jnp.dot(normed, w_v, preferred_element_type=jnp.float32)

    def mamba_piece(proj_arg, cw_arg, cb_arg, al_arg, ds_arg, db_arg, gm_arg):
        return mamba_mix(proj_arg, cw_arg, cb_arg, al_arg, ds_arg, db_arg, gm_arg, block_seg)
    mamba32, pull_mamba = jax.vjp(mamba_piece, projected, conv_weight, conv_bias, a_log, d_skip, dt_bias, g_mamba)
    mamba_out = mamba32.astype(jnp.bfloat16)

    def attn_piece(q_arg, k_arg, v_arg):
        return attend(q_arg, k_arg, v_arg, block_seg)
    attn32, pull_attn = jax.vjp(attn_piece, queries, keys_all, values_all)
    attn_out = attn32.astype(jnp.bfloat16)
    mixed = tok32 + mul_t(mamba_out, w_out) + mul_t(attn_out, w_o)
    hidden32, pull_norm_ff = jax.vjp(rms_norm, mixed, g_ff)
    hidden_norm = hidden32.astype(jnp.bfloat16)
    gate_pre = jnp.dot(hidden_norm, w_gate, preferred_element_type=jnp.float32)
    up_pre = jnp.dot(hidden_norm, w_up, preferred_element_type=jnp.float32)
    act32, pull_ffn = jax.vjp(swiglu, gate_pre, up_pre)
    act_ff = act32.astype(jnp.bfloat16)
    output = (mixed + mul_t(act_ff, w_down)).astype(jnp.bfloat16)
    d_act = jnp.dot(block_cot, w_down, preferred_element_type=jnp.float32)
    d_gate32, d_up32 = pull_ffn(d_act)
    d_gate = d_gate32.astype(jnp.bfloat16)
    d_up = d_up32.astype(jnp.bfloat16)
    d_hidden = mul_t(d_gate, w_gate) + mul_t(d_up, w_up)
    d_mixed_n, grad_g_ff = pull_norm_ff(d_hidden)
    d_mixed = block_cot.astype(jnp.float32) + d_mixed_n
    d_mixed_b = d_mixed.astype(jnp.bfloat16)
    d_mamba = jnp.dot(d_mixed_b, w_out, preferred_element_type=jnp.float32)
    d_attn = jnp.dot(d_mixed_b, w_o, preferred_element_type=jnp.float32)
    d_proj32, grad_cw, grad_cb, grad_al, grad_ds, grad_db, grad_gm = pull_mamba(d_mamba)
    d_q32, d_k32, d_v32 = pull_attn(d_attn)
    d_proj = d_proj32.astype(jnp.bfloat16)
    d_q = d_q32.astype(jnp.bfloat16)
    d_k = d_k32.astype(jnp.bfloat16)
    d_v = d_v32.astype(jnp.bfloat16)
    d_normed = mul_t(d_proj, w_in) + mul_t(d_q, w_q) + mul_t(d_k, w_k) + mul_t(d_v, w_v)
    d_tok_n, grad_g_in = pull_norm_in(d_normed)
    grad_tok = (d_mixed + d_tok_n).astype(jnp.bfloat16)
    big_grads = (t_mul(normed, d_proj), t_mul(normed, d_q), t_mul(normed, d_k), t_mul(normed, d_v), t_mul(d_mixed_b, attn_out), t_mul(d_mixed_b, mamba_out), t_mul(hidden_norm, d_gate), t_mul(hidden_norm, d_up), t_mul(block_cot, act_ff))
    small_grads = (grad_g_in, grad_g_ff, grad_gm, grad_cw, grad_cb, grad_al, grad_ds, grad_db)
    return (output, grad_tok, big_grads, small_grads)

def reference(tokens, segment_ids, cotangent, w_in, w_q, w_k, w_v, w_o, w_out, w_gate, w_up, w_down, g_in, g_ff, g_mamba, conv_weight, conv_bias, a_log, d_skip, dt_bias):
    blocks = N_FSDP * N_DP
    big = (w_in, w_q, w_k, w_v, w_o, w_out, w_gate, w_up, w_down)
    small = (g_in, g_ff, g_mamba, conv_weight, conv_bias, a_log, d_skip, dt_bias)
    tok_blocks = tokens.reshape(blocks, TOK_DEV, D)
    seg_blocks = segment_ids.reshape(blocks, TOK_DEV)
    cot_blocks = cotangent.reshape(blocks, TOK_DEV, D)
    init = (tuple((jnp.zeros(w.shape, jnp.float32) for w in big)), tuple((jnp.zeros(s.shape, jnp.float32) for s in small)))

    def scan_step(carry, inputs):
        block_tok, block_seg, block_cot = inputs
        output, grad_tok, big_grads, small_grads = layer_pass(block_tok, block_seg, block_cot, big, small)
        new_big = tuple((a + b for a, b in zip(carry[0], big_grads)))
        new_small = tuple((a + b for a, b in zip(carry[1], small_grads)))
        return ((new_big, new_small), (output, grad_tok))
    totals, outs_seq = lax.scan(scan_step, init, (tok_blocks, seg_blocks, cot_blocks))
    big_g, small_g = totals
    output = outs_seq[0].reshape(TOKENS, D)
    grad_tokens = outs_seq[1].reshape(TOKENS, D)
    return (output, grad_tokens, big_g[0], big_g[1], big_g[2], big_g[3], big_g[4], big_g[5], big_g[6], big_g[7], big_g[8], small_g[0], small_g[1], small_g[2], small_g[3], small_g[4], small_g[5], small_g[6], small_g[7])
```

```python
import functools
import math

import jax
import jax.numpy as jnp
from jax import lax
from jax.experimental import pallas as pl
from jax.experimental.pallas import tpu as pltpu
from jax.sharding import PartitionSpec as P


HD = 64
norm_eps = 1e-05
rope_base = 10000.0
HIGH = lax.Precision.HIGHEST
BF = jnp.bfloat16
F32 = jnp.float32


def mm(left, right):
    return jnp.dot(left, right, preferred_element_type=F32)


def mul_t(left, right):
    return lax.dot_general(left, right, (((1,), (1,)), ((), ())), preferred_element_type=F32)


def t_mul(left, right):
    return lax.dot_general(left, right, (((0,), (0,)), ((), ())), preferred_element_type=F32)


def cols(w, start, size):
    return lax.dynamic_slice(w, (0, start), (w.shape[0], size))


tie = lax.optimization_barrier


def next_peer(x):
    n = lax.axis_size("dp")
    return lax.ppermute(x, "dp", [(i, (i + 1) % n) for i in range(n)])


def peer_blocks(x):
    blocks = [x]
    for _ in range(lax.axis_size("dp") - 1):
        blocks.append(next_peer(blocks[-1]))
    return blocks


def peer_rows(x):
    return jnp.concatenate(peer_blocks(x), 0)


def peer_direct(x):
    n = lax.axis_size("dp")
    return [x] + [
        lax.ppermute(x, "dp", [(i, (i + k) % n) for i in range(n)]) for k in range(n - 1, 0, -1)
    ][::-1]


def flip(x, bits):
    size = lax.axis_size("fsdp")
    return lax.ppermute(x, "fsdp", [(i, i ^ bits) for i in range(size)])


def is_cube(width):
    return lax.axis_size("fsdp") == 8 and width % 1024 == 0


ORDER = (0, 2, 4, 6, 1, 3, 5, 7)


def gather_start(w):
    return [w] + [flip(w, m) for m in ORDER[1:4]]


def scatter_first(pairs):
    height = pairs[0][0].shape[1]
    return flip(grads(pairs, height // 2, height), 1)


def scatter_own(pairs, got):
    return grads(pairs, 0, pairs[0][0].shape[1] // 2, add=got, blocks=4)


def scatter_rest(own):
    return [own[0]] + [flip(own[i], ORDER[i]) for i in range(1, 4)]


def add_up(parts):
    total = parts[0].astype(F32)
    for p in parts[1:]:
        total = total + p.astype(F32)
    return total


def grad_kernel(count, add, blocks, *refs):
    total = []
    for left, right in zip(refs[:count], refs[count : 2 * count]):
        total.append(t_mul(left[...], right[...]))
    total = jnp.concatenate(total, 1)
    outs = refs[2 * count :]
    if add:
        total = total + outs[0][...].astype(F32)
        outs = outs[1:]
    total = total.astype(BF)
    if blocks == 1:
        outs[0][...] = total
        return
    for i in range(blocks):

        @pl.when(pl.program_id(0) == i)
        def _():
            outs[i][...] = total


def grads(pairs, low, high, add=None, blocks=1):
    depth = pairs[0][0].shape[0]
    height = high - low
    width = sum(r.shape[1] for _, r in pairs)
    rows = min(height, 256) if blocks == 1 else height // blocks
    first = low // rows
    if blocks == 1:
        out_shape = [jax.ShapeDtypeStruct((height, width), BF)]
        out_specs = [pl.BlockSpec((rows, width), lambda i: (i, 0))]
    else:
        out_shape = [jax.ShapeDtypeStruct((rows, width), BF)] * blocks
        out_specs = [pl.BlockSpec((rows, width), lambda i: (0, 0))] * blocks
    out = pl.pallas_call(
        functools.partial(grad_kernel, len(pairs), add is not None, blocks),
        out_shape=out_shape,
        grid=(height // rows,),
        in_specs=[pl.BlockSpec((depth, rows), lambda i: (0, i + first))] * len(pairs)
        + [pl.BlockSpec((depth, r.shape[1]), lambda i: (0, 0)) for _, r in pairs]
        + ([] if add is None else [pl.BlockSpec((rows, width), lambda i: (i, 0))]),
        out_specs=out_specs,
        cost_estimate=pl.CostEstimate(
            flops=2 * depth * height * width,
            bytes_accessed=2 * (depth * (height * len(pairs) + width) + height * width),
            transcendentals=0,
        ),
    )(*[l for l, _ in pairs], *[r for _, r in pairs], *([] if add is None else [add]))
    return out[0] if blocks == 1 else out


def reorder_kernel(back, count, at_ref, *refs):
    at = at_ref[0]
    for x_ref, o_ref in zip(refs[:count], refs[count:]):
        size = x_ref.shape[1] // 8
        for i, m in enumerate(ORDER):
            there = pl.ds(pl.multiple_of((at ^ m) * size, 128), size)
            here = pl.ds(i * size, size)
            if back:
                o_ref[:, there] = x_ref[:, here]
            else:
                o_ref[:, here] = x_ref[:, there]


def reorder(arrays, back=False):
    at = lax.axis_index("fsdp").astype(jnp.int32).reshape(1)
    vmem = pl.BlockSpec(memory_space=pltpu.VMEM)
    return pl.pallas_call(
        functools.partial(reorder_kernel, back, len(arrays)),
        out_shape=[jax.ShapeDtypeStruct(a.shape, a.dtype) for a in arrays],
        in_specs=[pl.BlockSpec(memory_space=pltpu.SMEM)] + [vmem] * len(arrays),
        out_specs=[vmem] * len(arrays),
    )(at, *arrays)


def lay_kernel(plan, n, kv_of, rank_ref, *refs):
    blocks, outs = refs[:n], refs[n:]
    rank = rank_ref[0]
    for kind, src, size, out, base in plan:
        o_ref = outs[out]
        if kind == "slice":
            for k in range(n):
                owner = lax.rem(rank - k + n, n)
                there = pl.ds(pl.multiple_of(base + owner * size, 128), size)
                o_ref[:, there] = blocks[k][:, src : src + size].astype(F32)
        elif kind == "sum":
            total = blocks[0][:, src : src + size].astype(F32)
            for k in range(1, n):
                total += blocks[k][:, src : src + size].astype(F32)
            o_ref[:, base : base + size] = total
        elif kind == "kv":
            heads = o_ref.shape[1] // size
            pieces = [jnp.zeros((o_ref.shape[0], size), F32)] * heads
            for k in range(n):
                owner = lax.rem(rank - k + n, n)
                value = blocks[k][:, src : src + size].astype(F32)
                for h in range(heads):
                    pieces[h] = pieces[h] + jnp.where(kv_of(owner) == h, value, 0.0)
            o_ref[...] = jnp.concatenate(pieces, 1)
        else:
            value = [blocks[k][:, src : src + size].astype(F32) for k in range(n)]
            for p in range(n):
                total = jnp.zeros_like(value[0])
                for k in range(n):
                    owner = lax.rem(rank - k + n, n)
                    total = jnp.where(owner == p, value[k], total)
                o_ref[:, base + p * size : base + (p + 1) * size] = total


def lay(blocks, plan, widths, kv_of):
    n = len(blocks)
    rank = lax.axis_index("dp").astype(jnp.int32).reshape(1)
    vmem = pl.BlockSpec(memory_space=pltpu.VMEM)
    return pl.pallas_call(
        functools.partial(lay_kernel, plan, n, kv_of),
        out_shape=[jax.ShapeDtypeStruct((blocks[0].shape[0], w), F32) for w in widths],
        in_specs=[pl.BlockSpec(memory_space=pltpu.SMEM)] + [vmem] * n,
        out_specs=[vmem] * len(widths),
    )(rank, *blocks)


def peer_send(blocks):
    n = lax.axis_size("dp")
    return [blocks[0]] + [
        lax.ppermute(blocks[k], "dp", [(i, (i - k) % n) for i in range(n)])
        for k in range(n - 1, 0, -1)
    ]


def peer_scalar_sum(v):
    n = lax.axis_size("dp")
    total = v
    for m in range(1, n):
        got = lax.ppermute(v, "dp", [(i, (i - m) % n) for i in range(n)])
        total = total + jnp.roll(got, -m, 0)
    return total


def sum_level(values):
    while len(values) > 1:
        values = [values[i] + values[i + 1] for i in range(0, len(values), 2)]
    return values[0]


def sum_dp(v):
    n = lax.axis_size("dp")
    if n & (n - 1):
        return lax.psum(v, "dp")
    got = [lax.ppermute(v, "dp", [(i, i ^ m) for i in range(n)]) for m in range(1, n)]
    return sum_level([v] + got)


def sum_fsdp(v):
    n, step = lax.axis_size("fsdp"), 1
    if n & (n - 1):
        return lax.psum(v, "fsdp")
    while step < n:
        v = v + lax.ppermute(v, "fsdp", [(i, i ^ step) for i in range(n)])
        step *= 2
    return v


def transposed(m):
    return jnp.swapaxes(m, 0, 1)


def column(row):
    size = row.shape[1]
    return transposed(jnp.broadcast_to(row, (size, size)))


def exact(a, b, dims):
    return lax.dot_general(a, b, (dims, ((), ())), precision=HIGH, preferred_element_type=F32)


def quick(a, b, dims):
    return lax.dot_general(
        a.astype(BF), b.astype(BF), (dims, ((), ())), preferred_element_type=F32
    )


NN, NT, TN = ((1,), (0,)), ((1,), (1,)), ((0,), (0,))


def shift_down(x, lag):
    return jnp.concatenate([jnp.zeros((lag, x.shape[1]), x.dtype), x[: x.shape[0] - lag]], 0)


def shift_up(x, lag):
    return jnp.concatenate([x[lag:], jnp.zeros((lag, x.shape[1]), x.dtype)], 0)


def branch_common(start, proj, conv_p, head_p, sizes):
    rows, inner, both, _ = sizes
    t_col = lax.broadcasted_iota(jnp.int32, (rows, rows), 0)
    s_row = lax.broadcasted_iota(jnp.int32, (rows, rows), 1)
    start_t = start.astype(F32)
    keep = (start_t == transposed(start_t)) & (s_row <= t_col)
    first = start_t[:, :1].astype(jnp.int32)
    t_one = t_col[:, :1]
    conv_in = proj[:, inner : 2 * inner + both]
    conv = conv_in * conv_p[3:4]
    lagged = []
    for lag in range(1, 4):
        ok = t_one - lag >= first
        moved = jnp.where(ok, shift_down(conv_in, lag), 0.0)
        lagged.append((ok, moved))
        conv = conv + moved * conv_p[3 - lag : 4 - lag]
    pre = conv + conv_p[4:5]
    gate = jax.nn.sigmoid(pre)
    act = pre * gate
    x, b, c = act[:, :inner], act[:, inner : inner + both // 2], act[:, inner + both // 2 :]
    dt = proj[:, proj.shape[1] - 128 :] + head_p[2:3]
    delta = jnp.maximum(dt, 0.0) + jnp.log1p(jnp.exp(-jnp.abs(dt)))
    decay_log = -delta * jnp.exp(head_p[0:1])
    lower = (s_row <= t_col).astype(F32)
    cum = exact(lower, decay_log, NN)
    cum_t, delta_t = transposed(cum), transposed(delta)
    scores = exact(c, b, NT)

    def head_decay(h):
        gap = cum[:, h : h + 1] - cum_t[h : h + 1]
        return jnp.where(keep, jnp.exp(jnp.where(keep, gap, 0.0)), 0.0)

    return dict(
        t_col=t_col, s_row=s_row, keep=keep, first=first, t_one=t_one, conv_in=conv_in,
        lagged=lagged, pre=pre, gate=gate, x=x, b=b, c=c, dt=dt, delta=delta,
        decay_log=decay_log, lower=lower, delta_t=delta_t, scores=scores, head_decay=head_decay,
    )


def swap_halves(x):
    lane = lax.broadcasted_iota(jnp.int32, x.shape, 1)
    size, half = x.shape[1], HD // 2
    low = lane % HD < half
    return jnp.where(low, pltpu.roll(x, size - half, 1), pltpu.roll(x, half, 1))


def rotary(first, rows):
    lane = lax.broadcasted_iota(jnp.int32, (rows, 128), 1)
    t = lax.broadcasted_iota(jnp.int32, (rows, 128), 0)
    half = HD // 2
    frequency = jnp.exp((lane % half).astype(F32) * (-2.0 / HD * math.log(rope_base)))
    angle = (t - first).astype(F32) * frequency
    return jnp.cos(angle), jnp.where(lane % HD < half, -jnp.sin(angle), jnp.sin(angle))


def attn_common(q, kv, first, keep):
    rows = q.shape[0]
    lane = lax.broadcasted_iota(jnp.int32, (rows, 128), 1)
    low = lane < HD
    cosine, sine = rotary(first, rows)
    q_rot = q * cosine + swap_halves(q) * sine
    k_rot = kv * cosine + swap_halves(kv) * sine
    keys = jnp.where(low, k_rot, pltpu.roll(k_rot, HD, 1))
    values = jnp.where(low, pltpu.roll(kv, HD, 1), kv)
    probs, picks = [], []
    for h in range(2):
        pick = low if h == 0 else ~low
        logits = exact(jnp.where(pick, q_rot, 0.0), keys, NT) * HD ** (-0.5)
        logits = jnp.where(keep, logits, -1e30)
        expo = jnp.exp(logits - jnp.max(logits, -1, keepdims=True))
        probs.append(expo / jnp.sum(expo, -1, keepdims=True))
        picks.append(pick)
    return low, cosine, sine, q_rot, keys, values, probs, picks


def branch_forward(
    sizes, q_at, x_ref, a0_ref, a1_ref, g_ref, conv_ref, head_ref,
    normed_ref, proj_ref, y_ref, gated_ref, square_ref, attn_ref,
):
    rows, inner, _, heads = sizes
    width = g_ref.shape[1]
    x32 = x_ref[:, :width].astype(F32)
    scale = lax.rsqrt(jnp.mean(x32 * x32, -1, keepdims=True) + norm_eps)
    normed = (x32 * scale * g_ref[...]).astype(BF)
    normed_ref[...] = normed
    half = a0_ref.shape[0]
    proj = mm(normed[:, :half], a0_ref[...]) + mm(normed[:, half:], a1_ref[...])
    proj_ref[...] = proj
    start = x_ref[:, width:]
    conv_p, head_p = conv_ref[...], head_ref[...]
    v = branch_common(start, proj, conv_p, head_p, sizes)
    low = v["s_row"] < HD
    outs = []
    for pair in range(heads // 2):
        x_pair = v["x"][:, pair * 128 : pair * 128 + 128]
        y = []
        for h in (2 * pair, 2 * pair + 1):
            mixer = v["scores"] * v["head_decay"](h) * v["delta_t"][h : h + 1]
            y.append(quick(mixer, x_pair, NN))
        outs.append(jnp.where(low, y[0], y[1]))
    y = jnp.concatenate(outs, 1) + conv_p[5:6, :inner] * v["x"]
    z = proj[:, :inner]
    gated = y * (z * jax.nn.sigmoid(z))
    y_ref[...] = y
    gated_ref[...] = gated
    square = jnp.sum(gated * gated, -1, keepdims=True)
    square_ref[0] = transposed(jnp.broadcast_to(square, (rows, rows)))[:1]
    q, kv = proj[:, q_at : q_at + 128], proj[:, q_at + 128 : q_at + 256]
    low, _, _, _, _, values, probs, _ = attn_common(q, kv, v["first"], v["keep"])
    out = [quick(p, values, NN) for p in probs]
    attn_ref[...] = jnp.where(low, out[0], out[1]).astype(BF)


def branch_back_out(
    sizes, low, dm_ref, b0_ref, b1_ref, gated_ref, scale_ref, gm_ref,
    d_scaled_ref, d_attn_ref, inner_ref, g_gm_ref,
):
    rows, inner, _, _ = sizes
    d_mix = halved(dm_ref[...], b0_ref[:, low:], b1_ref[:, low:])
    d_out = d_mix[:, :inner]
    gated = gated_ref[...]
    scale = column(scale_ref[0])[:, :1]

    @pl.when(pl.program_id(0) == 0)
    def _():
        g_gm_ref[...] = jnp.zeros_like(g_gm_ref)

    g_gm_ref[...] += jnp.sum(d_out * gated * scale, 0, keepdims=True)
    d_scaled = d_out * gm_ref[...]
    d_scaled_ref[...] = d_scaled
    dot = jnp.sum(d_scaled * gated, -1, keepdims=True)
    inner_ref[0] = transposed(jnp.broadcast_to(dot, (rows, rows)))[:1]
    d_attn_ref[...] = d_mix[:, inner:]


def branch_back_attn(q_at, x_ref, proj_ref, d_attn_ref, d_qkv_ref):
    start = x_ref[...].astype(F32)
    rows = start.shape[0]
    t_col = lax.broadcasted_iota(jnp.int32, (rows, rows), 0)
    s_row = lax.broadcasted_iota(jnp.int32, (rows, rows), 1)
    keep = (start == transposed(start)) & (s_row <= t_col)
    first = start[:, :1].astype(jnp.int32)
    q = proj_ref[:, q_at : q_at + 128]
    kv = proj_ref[:, q_at + 128 : q_at + 256]
    low, cosine, sine, q_rot, keys, values, probs, picks = attn_common(q, kv, first, keep)
    d_attn = d_attn_ref[...]
    d_q = []
    d_k = jnp.zeros((rows, 128), F32)
    d_v = jnp.zeros((rows, 128), F32)
    for p, pick in zip(probs, picks):
        d_head = jnp.where(pick, d_attn, 0.0)
        d_p = quick(d_head, values, NT)
        d_logit = p * (d_p - jnp.sum(d_p * p, -1, keepdims=True)) * HD ** (-0.5)
        d_q.append(quick(d_logit, keys, NN))
        d_k += quick(d_logit, jnp.where(pick, q_rot, 0.0), TN)
        d_v += quick(p, d_head, TN)
    d_q = jnp.where(low, d_q[0], d_q[1])
    d_k = d_k + pltpu.roll(d_k, HD, 1)
    d_v = d_v + pltpu.roll(d_v, HD, 1)
    d_q = d_q * cosine + swap_halves(d_q * sine)
    d_k = d_k * cosine + swap_halves(d_k * sine)
    d_qkv_ref[:, :128] = d_q.astype(BF)
    d_qkv_ref[:, 128:] = jnp.where(low, d_k, d_v).astype(BF)


def branch_back_mamba(
    sizes, q_at, x_ref, proj_ref, y_ref, gated_ref, d_scaled_ref, scale_ref, inner_ref,
    d_qkv_ref, conv_ref, head_ref, whole,
    d_proj_ref, g_conv_ref, g_head_ref, g_skip_ref,
):
    rows, inner, both, heads = sizes

    @pl.when(pl.program_id(0) == 0)
    def _():
        g_conv_ref[...] = jnp.zeros_like(g_conv_ref)
        g_head_ref[...] = jnp.zeros_like(g_head_ref)
        g_skip_ref[...] = jnp.zeros_like(g_skip_ref)

    proj = proj_ref[...]
    conv_p, head_p = conv_ref[...], head_ref[...]
    v = branch_common(x_ref[...], proj, conv_p, head_p, sizes)
    scale = column(scale_ref[0])[:, :1]
    dot = column(inner_ref[0])[:, :1]
    d_gated = scale * d_scaled_ref[...] - gated_ref[...] * (scale * scale * scale * dot / whole)
    z = proj[:, :inner]
    zs = jax.nn.sigmoid(z)
    d_y = d_gated * (z * zs)
    d_z = d_gated * y_ref[...] * (zs * (1.0 + z * (1.0 - zs)))
    d_proj_ref[:, :inner] = d_z.astype(BF)
    x, scores, delta_t = v["x"], v["scores"], v["delta_t"]
    g_skip_ref[...] += jnp.sum(d_y * x, 0, keepdims=True)
    low = v["s_row"] < HD
    d_x = []
    d_scores = jnp.zeros((rows, rows), F32)
    d_cum = jnp.zeros((rows, rows), F32)
    d_delta_rows, d_cum_rows = [], []
    for pair in range(heads // 2):
        at = slice(pair * 128, pair * 128 + 128)
        x_pair, dy_pair = x[:, at], d_y[:, at]
        parts = []
        for h in (2 * pair, 2 * pair + 1):
            pick = low if h % 2 == 0 else ~low
            decay = v["head_decay"](h)
            scored = scores * decay
            mixer = scored * delta_t[h : h + 1]
            d_mixer = quick(jnp.where(pick, dy_pair, 0.0), x_pair, NT)
            parts.append(quick(mixer, dy_pair, TN))
            d_scores += d_mixer * (decay * delta_t[h : h + 1])
            d_delta_rows.append(jnp.sum(d_mixer * scored, 0, keepdims=True))
            flow = d_mixer * mixer
            d_cum_rows.append(jnp.sum(flow, 0, keepdims=True))
            d_cum = jnp.where(v["s_row"] == h, jnp.sum(flow, -1, keepdims=True), d_cum)
        d_x.append(jnp.where(low, parts[0], parts[1]))
    blank = jnp.zeros((rows - heads, rows), F32)
    d_delta = transposed(jnp.concatenate(d_delta_rows + [blank], 0))
    d_cum = d_cum - transposed(jnp.concatenate(d_cum_rows + [blank], 0))
    d_log = exact(v["lower"], d_cum, TN)
    d_delta = d_delta - jnp.exp(head_p[0:1]) * d_log
    d_dt = d_delta * jax.nn.sigmoid(v["dt"])
    g_head_ref[0:1] += jnp.sum(d_log * v["decay_log"], 0, keepdims=True)
    g_head_ref[1:2] += jnp.sum(d_dt, 0, keepdims=True)
    d_proj_ref[:, d_proj_ref.shape[1] - 128 :] = d_dt.astype(BF)
    d_act = jnp.concatenate(
        d_x + [quick(d_scores, v["c"], TN), quick(d_scores, v["b"], NN)], 1
    )
    d_act = jnp.concatenate(
        [d_act[:, :inner] + conv_p[5:6, :inner] * d_y, d_act[:, inner:]], 1
    )
    gate = v["gate"]
    d_conv = d_act * (gate * (1.0 + v["pre"] * (1.0 - gate)))
    g_conv_ref[4:5] += jnp.sum(d_conv, 0, keepdims=True)
    g_conv_ref[3:4] += jnp.sum(d_conv * v["conv_in"], 0, keepdims=True)
    d_in = d_conv * conv_p[3:4]
    for lag, (ok, moved) in zip(range(1, 4), v["lagged"]):
        g_conv_ref[3 - lag : 4 - lag] += jnp.sum(d_conv * moved, 0, keepdims=True)
        back = shift_up(jnp.where(ok, d_conv, 0.0), lag)
        d_in = d_in + back * conv_p[3 - lag : 4 - lag]
    d_proj_ref[:, inner : 2 * inner + both] = d_in.astype(BF)
    d_proj_ref[:, q_at : q_at + 256] = d_qkv_ref[...]


def halved(left, w0, w1):
    half = w0.shape[0]
    return mm(left[:, :half], w0) + mm(left[:, half:], w1)


def put_rows(outs, left, w0, w1):
    value = jnp.concatenate([mul_t(left, w0), mul_t(left, w1)], 1)
    for k, o_ref in enumerate(outs):

        @pl.when(pl.program_id(0) == k)
        def _():
            o_ref[...] = value.astype(o_ref.dtype)


def rows_out(n, rows, width):
    spec = pl.BlockSpec((rows, width), lambda i: (0, 0))
    shapes = [out_of((rows, width), F32)] + [out_of((rows, width), BF)] * (n - 1)
    return [spec] * n, shapes


def rows_kernel(low, high, left_ref, w0_ref, w1_ref, *outs):
    put_rows(outs, left_ref[...], w0_ref[:, low:high], w1_ref[:, low:high])


def partial_rows(n, left, halves, low, high):
    rows, width = left.shape[0] // n, 2 * halves[0].shape[0]
    specs, shapes = rows_out(n, rows, width)
    return pl.pallas_call(
        functools.partial(rows_kernel, low, high),
        grid=(n,),
        in_specs=[row_spec(rows, left.shape[1])] + [fixed_spec(a) for a in halves],
        out_specs=specs,
        out_shape=shapes,
    )(left, *halves)


def mix_kernel(low, gated_ref, scale_ref, gm_ref, attn_ref, w0_ref, w1_ref, mix_ref, *outs):
    scale = column(scale_ref[0])[:, :1]
    mamba = (gated_ref[...] * scale * gm_ref[...]).astype(BF)
    mix = jnp.concatenate([mamba, attn_ref[...]], 1)
    mix_ref[...] = mix
    put_rows(outs, mix, w0_ref[:, low:], w1_ref[:, low:])


def ffn_kernel(size, hid_ref, cot_ref, w0_ref, w1_ref, act_ref, d_gu_ref, *outs):
    gu = halved(hid_ref[...], w0_ref[:, : 2 * size], w1_ref[:, : 2 * size])
    gate, up = gu[:, :size], gu[:, size:]
    sig = jax.nn.sigmoid(gate)
    silu = gate * sig
    act_ref[...] = (silu * up).astype(BF)
    d_act = halved(cot_ref[...], w0_ref[:, 2 * size :], w1_ref[:, 2 * size :])
    d_gate = d_act * up * (sig * (1.0 + gate * (1.0 - sig)))
    d_gu = jnp.concatenate([d_gate.astype(BF), (d_act * silu).astype(BF)], 1)
    d_gu_ref[...] = d_gu
    put_rows(outs, d_gu, w0_ref[:, : 2 * size], w1_ref[:, : 2 * size])


def row_spec(*shape):
    return pl.BlockSpec(shape, lambda i: (i,) + (0,) * (len(shape) - 1))


def fixed_spec(a):
    return pl.BlockSpec(a.shape, lambda i: (0,) * len(a.shape))


def out_of(shape, dtype):
    return jax.ShapeDtypeStruct(shape, dtype)


def rms_scale(x):
    return lax.rsqrt(jnp.mean(x * x, -1, keepdims=True) + norm_eps)


def rms_back(x, scale, gain, d_out):
    scaled = d_out * gain
    inner = jnp.mean(scaled * x, -1, keepdims=True)
    return scale * scaled - x * (scale * scale * scale * inner), jnp.sum(d_out * x * scale, 0)


def body(
    tokens,
    segment_ids,
    cotangent,
    w_in,
    w_q,
    w_k,
    w_v,
    w_o,
    w_out,
    w_gate,
    w_up,
    w_down,
    g_in,
    g_ff,
    g_mamba,
    conv_weight,
    conv_bias,
    a_log,
    d_skip,
    dt_bias,
):
    n = lax.axis_size("dp")
    rank = lax.axis_index("dp")
    rows, width = tokens.shape
    inner, channels, heads = g_mamba.shape[0], conv_bias.shape[0], a_log.shape[0]
    hidden = w_gate.shape[1]
    q_heads, kv_heads = w_q.shape[1] // HD, w_k.shape[1] // HD
    my_inner, my_heads, my_hidden, my_q = inner // n, heads // n, hidden // n, q_heads // n
    per_kv = q_heads // kv_heads
    assert heads % n == 0 and q_heads % n == 0 and hidden % n == 0 and per_kv % my_q == 0
    kv = rank * my_q // per_kv
    both = channels - inner
    qc = my_q * HD

    cube = is_cube(width)
    tail_pad = -my_heads % 128
    assert rows <= 256
    start = (segment_ids - segment_ids[0]).astype(BF)
    start = jnp.broadcast_to(start[:, None], (rows, 128))
    sh_a = jnp.concatenate(
        [
            cols(w_in, rank * my_inner, my_inner),
            cols(w_in, inner + rank * my_inner, my_inner),
            w_in[:, 2 * inner : inner + channels],
            cols(w_q, rank * qc, qc),
            cols(w_k, kv * HD, HD),
            cols(w_v, kv * HD, HD),
            cols(w_in, inner + channels + rank * my_heads, my_heads),
            jnp.zeros((w_in.shape[0], tail_pad), BF),
            cols(w_out, rank * my_inner, my_inner),
            cols(w_o, rank * qc, qc),
        ],
        1,
    )
    sh_a, tokens, start = tie((sh_a, tokens, start))
    if cube:
        parts_a = gather_start(sh_a)
        tokens, cotangent, g_in, g_ff = reorder(
            [tokens, cotangent, g_in.reshape(1, width), g_ff.reshape(1, width)]
        )
    first = peer_rows(jnp.concatenate([tokens, start], 1))
    if cube:
        parts_a, first = tie((parts_a, first))
        own_a = jnp.concatenate(parts_a, 0)
        halves_a = [own_a, flip(own_a, 1)]
    else:
        full_a = lax.all_gather(sh_a, "fsdp", axis=0, tiled=True)
        halves_a = [full_a[: width // 2], full_a[width // 2 :]]

    sh_b = jnp.concatenate(
        [cols(w, rank * my_hidden, my_hidden) for w in (w_gate, w_up, w_down)], 1
    )
    if cube:
        sh_b, parts_a = tie((sh_b, parts_a))
        parts_b = gather_start(sh_b)
    cot_first, _ = tie((cotangent, first))
    cot_blocks = peer_direct(cot_first)

    o = 2 * my_inner + both
    mc = my_inner + qc
    span = sh_a.shape[1] - mc
    assert rows == 128 and qc == 128 and 2 * HD == 128 and conv_weight.shape[0] == 4
    assert my_heads % 2 == 0 and both % 256 == 0 and inner // heads == HD
    cw = jnp.concatenate(
        [cols(conv_weight, rank * my_inner, my_inner), conv_weight[:, inner:]], 1
    )
    cb = jnp.concatenate(
        [lax.dynamic_slice(conv_bias, (rank * my_inner,), (my_inner,)), conv_bias[inner:]]
    )

    def mine(p, size):
        return lax.dynamic_slice(p, (rank * size,), (size,))

    gm = mine(g_mamba, my_inner)

    sizes = (rows, my_inner, both, my_heads)
    skip = jnp.repeat(mine(d_skip, my_heads), HD)
    conv_p = jnp.concatenate(
        [cw, cb[None], jnp.pad(skip, (0, both))[None], jnp.zeros((2, cw.shape[1]), F32)], 0
    )
    head_p = jnp.stack(
        [mine(a_log, my_heads), mine(d_skip, my_heads), mine(dt_bias, my_heads)], 0
    )
    head_p = jnp.pad(head_p, ((0, 5), (0, 128 - my_heads)))
    gm = gm.reshape(1, my_inner)
    g_in_row = g_in.reshape(1, width)
    count = n * rows
    normed, proj, y, gated, square, attn = pl.pallas_call(
        functools.partial(branch_forward, sizes, o),
        grid=(n,),
        in_specs=[row_spec(rows, first.shape[1])]
        + [pl.BlockSpec((a.shape[0], span), lambda i: (0, 0)) for a in halves_a]
        + [fixed_spec(a) for a in (g_in_row, conv_p, head_p)],
        out_specs=[
            row_spec(rows, width),
            row_spec(rows, span),
            row_spec(rows, my_inner),
            row_spec(rows, my_inner),
            row_spec(1, 1, rows),
            row_spec(rows, qc),
        ],
        out_shape=[
            out_of((count, width), BF),
            out_of((count, span), F32),
            out_of((count, my_inner), F32),
            out_of((count, my_inner), F32),
            out_of((n, 1, rows), F32),
            out_of((count, qc), BF),
        ],
    )(first, *halves_a, g_in_row, conv_p, head_p)
    square = peer_scalar_sum(square.reshape(n, rows))
    scale_rows = lax.rsqrt(square / inner + norm_eps).reshape(n, 1, rows)
    specs, shapes = rows_out(n, rows, width)
    mix_in, *mix_parts = pl.pallas_call(
        functools.partial(mix_kernel, span),
        grid=(n,),
        in_specs=[row_spec(rows, my_inner), row_spec(1, 1, rows), fixed_spec(gm)]
        + [row_spec(rows, qc)]
        + [fixed_spec(a) for a in halves_a],
        out_specs=[row_spec(rows, mc)] + specs,
        out_shape=[out_of((count, mc), BF)] + shapes,
    )(gated, scale_rows, gm, attn, *halves_a)
    mix_parts = peer_send(mix_parts)
    if cube:
        mix_parts, parts_b, cot_blocks = tie((mix_parts, parts_b, cot_blocks))
        own_b = jnp.concatenate(parts_b, 0)
        halves_b = [own_b, flip(own_b, 1)]
    else:
        full_b = lax.all_gather(sh_b, "fsdp", axis=0, tiled=True)
        halves_b = [full_b[: width // 2], full_b[width // 2 :]]
    cot_all = jnp.concatenate(cot_blocks, 0)
    tok32 = tokens.astype(F32)
    mixed = tok32 + add_up(mix_parts)
    f_scale = rms_scale(mixed)
    hid_all = peer_rows((mixed * f_scale * g_ff).astype(BF))
    act, d_gu, *d_hidden = pl.pallas_call(
        functools.partial(ffn_kernel, my_hidden),
        grid=(n,),
        in_specs=[row_spec(rows, width)] * 2 + [fixed_spec(a) for a in halves_b],
        out_specs=[row_spec(rows, my_hidden), row_spec(rows, 2 * my_hidden)] + specs,
        out_shape=[out_of((count, my_hidden), BF), out_of((count, 2 * my_hidden), BF)]
        + shapes,
    )(hid_all, cot_all, *halves_b)
    d_hidden = peer_send(d_hidden)
    c_pairs = [(hid_all, d_gu), (cot_all, act)]
    if cube:
        c_own = scatter_own(c_pairs, scatter_first(c_pairs))
        grad_c = scatter_rest(c_own)
        d_hidden, c_own = tie((d_hidden, c_own))
    else:
        grad_c = grads(c_pairs, 0, width)
    d_mixed_n, grad_g_ff = rms_back(mixed, f_scale, g_ff, add_up(d_hidden))
    d_mixed = cotangent.astype(F32) + d_mixed_n
    dm_all = peer_rows(d_mixed.astype(BF))
    dm_all, grad_c = tie((dm_all, grad_c))
    if cube:
        grad_c = add_up(grad_c).astype(BF)
    else:
        grad_c = lax.psum_scatter(grad_c, "fsdp", scatter_dimension=0, tiled=True)
    start_all = first[:, width:]
    c_blocks = peer_direct(grad_c)
    d_scaled, d_attn, m_inner, grad_gm = pl.pallas_call(
        functools.partial(branch_back_out, sizes, span),
        grid=(n,),
        in_specs=[row_spec(rows, width)]
        + [fixed_spec(a) for a in halves_a]
        + [row_spec(rows, my_inner), row_spec(1, 1, rows), fixed_spec(gm)],
        out_specs=[
            row_spec(rows, my_inner),
            row_spec(rows, qc),
            row_spec(1, 1, rows),
            fixed_spec(gm),
        ],
        out_shape=[
            out_of((count, my_inner), F32),
            out_of((count, qc), F32),
            out_of((n, 1, rows), F32),
            out_of((1, my_inner), F32),
        ],
    )(dm_all, *halves_a, gated, scale_rows, gm)
    act, d_attn, m_inner = tie((act, d_attn, m_inner))
    d_qkv = pl.pallas_call(
        functools.partial(branch_back_attn, o),
        grid=(n,),
        in_specs=[row_spec(rows, rows), row_spec(rows, span), row_spec(rows, qc)],
        out_specs=row_spec(rows, 256),
        out_shape=out_of((count, 256), BF),
        cost_estimate=pl.CostEstimate(
            flops=30 * count * rows * 128, bytes_accessed=count * 5000, transcendentals=count * 512
        ),
    )(start_all, proj, d_attn)
    m_inner = peer_scalar_sum(m_inner.reshape(n, rows)).reshape(n, 1, rows)
    act, _ = tie((act, d_qkv))
    out_parts = partial_rows(n, act, halves_b, 2 * my_hidden, 3 * my_hidden)
    out_parts = peer_send(out_parts)
    m_inner, d_qkv, c_blocks = tie((m_inner, d_qkv, c_blocks))
    d_proj, g_conv, g_head, g_skip = pl.pallas_call(
        lambda *refs: branch_back_mamba(sizes, o, *refs[:10], float(inner), *refs[10:]),
        grid=(n,),
        in_specs=[
            row_spec(rows, rows),
            row_spec(rows, span),
            row_spec(rows, my_inner),
            row_spec(rows, my_inner),
            row_spec(rows, my_inner),
            row_spec(1, 1, rows),
            row_spec(1, 1, rows),
            row_spec(rows, 256),
            fixed_spec(conv_p),
            fixed_spec(head_p),
        ],
        out_specs=[
            row_spec(rows, span),
            fixed_spec(conv_p),
            fixed_spec(head_p),
            fixed_spec(gm),
        ],
        out_shape=[
            out_of((count, span), BF),
            out_of(conv_p.shape, F32),
            out_of(head_p.shape, F32),
            out_of((1, my_inner), F32),
        ],
    )(start_all, proj, y, gated, d_scaled, scale_rows, m_inner, d_qkv, conv_p, head_p)
    a_pairs = [(dm_all, mix_in), (normed, d_proj)]
    if cube:
        got = scatter_first(a_pairs)
        d_proj, _ = tie((d_proj, a_pairs))
    d_normed = partial_rows(n, d_proj, halves_a, 0, span)
    if cube:
        own = scatter_own(a_pairs, got)
        grad_a = scatter_rest(own)
        d_normed, out_parts, own = tie((d_normed, out_parts, own))
        d_normed = peer_send(d_normed)
        grad_a = add_up(grad_a).astype(BF)
    else:
        d_normed = peer_send(d_normed)
        grad_a = lax.psum_scatter(
            grads(a_pairs, 0, width), "fsdp", scatter_dimension=0, tiled=True
        )
    output = (mixed + add_up(out_parts)).astype(BF)
    d_tok_n, grad_g_in = rms_back(tok32, rms_scale(tok32), g_in, add_up(d_normed))
    grad_tokens = (d_mixed + d_tok_n).astype(BF)
    if cube:
        output, grad_tokens = reorder([output, grad_tokens], back=True)

    def place(v):
        spot = (jnp.arange(n) == rank).astype(F32)
        spread = spot[:, None, None] * v.reshape(v.shape[:-1] + (1, -1, 128))
        return spread.reshape(-1, 128)

    def ordered(v):
        v = v.reshape(-1, 128)
        if not cube:
            return v
        block = jnp.array(ORDER) ^ lax.axis_index("fsdp")
        hit = (jnp.arange(8)[:, None] == block[None, :]).astype(F32)
        v = v.reshape(8, 1, -1)
        return jnp.sum(hit.T[:, :, None] * v, 0).reshape(-1, 128)

    def head_row(v):
        spot = (jnp.arange(n) == rank).astype(F32)
        return jnp.pad((spot[:, None] * v[None]).reshape(1, -1), ((0, 0), (0, 128 - heads)))

    grad_gm, g_cw, g_cb = grad_gm[0], g_conv[:4], g_conv[4]
    g_al, g_db = g_head[0, :my_heads], g_head[1, :my_heads]
    g_ds = jnp.sum(g_skip.reshape(my_heads, HD), 1)
    small = [ordered(grad_g_in), ordered(grad_g_ff), place(grad_gm)]
    for row in range(g_cw.shape[0]):
        small += [place(g_cw[row, :my_inner]), g_cw[row, my_inner:].reshape(-1, 128)]
    small += [place(g_cb[:my_inner]), g_cb[my_inner:].reshape(-1, 128)]
    small += [head_row(g_al), head_row(g_ds), head_row(g_db)]
    flat = jnp.concatenate(small)
    flat = jnp.pad(flat, ((0, -flat.shape[0] % 8), (0, 0)))
    flat, grad_a = tie((sum_dp(flat), grad_a))
    a_blocks = peer_blocks(grad_a)
    flat = sum_fsdp(flat)

    def kv_of(owner):
        return owner * my_q // per_kv

    grad_gate, grad_up, grad_down = lay(
        c_blocks,
        [("slice", i * my_hidden, my_hidden, i, 0) for i in range(3)],
        [hidden] * 3,
        kv_of,
    )
    grad_in, grad_q, grad_k, grad_v, grad_out, grad_o = lay(
        a_blocks,
        [
            ("slice", 0, my_inner, 4, 0),
            ("slice", my_inner, qc, 5, 0),
            ("slice", mc, my_inner, 0, 0),
            ("slice", mc + my_inner, my_inner, 0, inner),
            ("sum", mc + 2 * my_inner, both, 0, 2 * inner),
            ("slice", mc + o, qc, 1, 0),
            ("kv", mc + o + qc, HD, 2, 0),
            ("kv", mc + o + qc + HD, HD, 3, 0),
            ("tail", mc + o + qc + 2 * HD, my_heads, 0, inner + channels),
        ],
        [w_in.shape[1], w_q.shape[1], w_k.shape[1], w_v.shape[1], inner, w_o.shape[1]],
        kv_of,
    )

    sizes = [width, width, inner, g_cw.shape[0] * channels, channels]
    sums, at = [], 0
    for size in sizes:
        sums.append(flat[at : at + size // 128].reshape(-1))
        at += size // 128
    for i in range(3):
        sums.append(flat[at + i, :heads])
    return (
        output,
        grad_tokens,
        grad_in,
        grad_q,
        grad_k,
        grad_v,
        grad_o,
        grad_out,
        grad_gate,
        grad_up,
        grad_down,
        sums[0],
        sums[1],
        sums[2],
        sums[3].reshape(conv_weight.shape),
        sums[4],
        sums[5],
        sums[6],
        sums[7],
    )


def solution(mesh):
    rows, shard, whole = P(("fsdp", "dp"), None), P("fsdp", None), P()
    in_specs = (rows, P(("fsdp", "dp")), rows) + (shard,) * 9 + (whole,) * 8
    out_specs = (rows, rows) + (shard,) * 9 + (whole,) * 8

    return jax.shard_map(body, mesh=mesh, in_specs=in_specs, out_specs=out_specs, check_vma=False)
```

```python
import functools
import math

import jax
import jax.numpy as jnp
from jax import lax
from jax.experimental import pallas as pl
from jax.experimental.pallas import tpu as pltpu
from jax.sharding import PartitionSpec as P


HD = 64
norm_eps = 1e-05
rope_base = 10000.0
HIGH = lax.Precision.HIGHEST
BF = jnp.bfloat16
F32 = jnp.float32


def mm(left, right):
    return jnp.dot(left, right, preferred_element_type=F32)


def mul_t(left, right):
    return lax.dot_general(left, right, (((1,), (1,)), ((), ())), preferred_element_type=F32)


def t_mul(left, right):
    return lax.dot_general(left, right, (((0,), (0,)), ((), ())), preferred_element_type=F32)


def cols(w, start, size):
    return lax.dynamic_slice(w, (0, start), (w.shape[0], size))


tie = lax.optimization_barrier


def next_peer(x):
    n = lax.axis_size("dp")
    return lax.ppermute(x, "dp", [(i, (i + 1) % n) for i in range(n)])


def peer_blocks(x):
    blocks = [x]
    for _ in range(lax.axis_size("dp") - 1):
        blocks.append(next_peer(blocks[-1]))
    return blocks


def peer_direct(x):
    n = lax.axis_size("dp")
    return [x] + [
        lax.ppermute(x, "dp", [(i, (i + k) % n) for i in range(n)]) for k in range(n - 1, 0, -1)
    ][::-1]


def flip(x, bits):
    size = lax.axis_size("fsdp")
    return lax.ppermute(x, "fsdp", [(i, i ^ bits) for i in range(size)])


def is_cube(width):
    return lax.axis_size("fsdp") == 8 and width % 1024 == 0


ORDER = (0, 2, 4, 6, 1, 3, 5, 7)


def gather_start(w):
    return [w] + [flip(w, m) for m in ORDER[1:4]]


def scatter_first(pairs):
    height = pairs[0][0].shape[1]
    return flip(grads(pairs, height // 2, height), 1)


def scatter_own(pairs, got):
    return grads(pairs, 0, pairs[0][0].shape[1] // 2, add=got, blocks=4)


def scatter_rest(own):
    return [own[0]] + [flip(own[i], ORDER[i]) for i in range(1, 4)]


def add_up(parts):
    total = parts[0].astype(F32)
    for p in parts[1:]:
        total = total + p.astype(F32)
    return total


def grad_kernel(count, add, blocks, *refs):
    total = []
    for left, right in zip(refs[:count], refs[count : 2 * count]):
        total.append(t_mul(left[...], right[...]))
    total = jnp.concatenate(total, 1)
    outs = refs[2 * count :]
    if add:
        total = total + outs[0][...].astype(F32)
        outs = outs[1:]
    total = total.astype(BF)
    rows = total.shape[0] // blocks
    for i in range(blocks):
        outs[i][...] = total[i * rows : (i + 1) * rows]


def grads(pairs, low, high, add=None, blocks=1):
    depth = pairs[0][0].shape[0]
    height = high - low
    width = sum(r.shape[1] for _, r in pairs)
    rows = height // blocks
    out_shape = [jax.ShapeDtypeStruct((rows, width), BF)] * blocks
    out_specs = [pl.BlockSpec((rows, width), lambda i: (0, 0))] * blocks
    out = pl.pallas_call(
        functools.partial(grad_kernel, len(pairs), add is not None, blocks),
        out_shape=out_shape,
        grid=(1,),
        in_specs=[pl.BlockSpec((depth, height), lambda i: (0, low // height))] * len(pairs)
        + [pl.BlockSpec((depth, r.shape[1]), lambda i: (0, 0)) for _, r in pairs]
        + ([] if add is None else [pl.BlockSpec((height, width), lambda i: (0, 0))]),
        out_specs=out_specs,
        cost_estimate=pl.CostEstimate(
            flops=2 * depth * height * width,
            bytes_accessed=2 * (depth * (height * len(pairs) + width) + height * width),
            transcendentals=0,
        ),
    )(*[l for l, _ in pairs], *[r for _, r in pairs], *([] if add is None else [add]))
    return out[0] if blocks == 1 else out


def slice_kernel(dims, rank_ref, *refs):
    inner, channels, my_inner, my_heads, my_hidden, qc, my_q, per_kv, n = dims
    w_in, w_q, w_k, w_v, w_o, w_out, w_gate, w_up, w_down, ab_ref, cd_ref = refs
    rank = rank_ref[0]
    kv = rank * my_q // per_kv

    def wide(base, size):
        return jnp.swapaxes(w_in[pl.ds(pl.multiple_of(base, 128), size), :], 0, 1)

    def piece(ref, base, size):
        return ref[:, pl.ds(pl.multiple_of(base + rank * size, 128), size)]

    def pick(ref, base, size, which, count):
        value = ref[:, base : base + size].astype(F32)
        for i in range(1, count):
            at = base + i * size
            value = jnp.where(which == i, ref[:, at : at + size].astype(F32), value)
        return value

    heads = w_k.shape[1] // HD
    dt_at = inner + channels
    tail = w_in[dt_at : dt_at + n * my_heads, :].astype(F32)
    tail = jnp.concatenate([tail, jnp.zeros((128 - n * my_heads, tail.shape[1]), F32)], 0)
    tail = jnp.swapaxes(tail, 0, 1)
    dt = tail[:, :my_heads]
    for i in range(1, n):
        dt = jnp.where(rank == i, tail[:, i * my_heads : (i + 1) * my_heads], dt)
    blank = jnp.zeros((dt.shape[0], -my_heads % 128), F32)
    parts = [
        wide(rank * my_inner, my_inner),
        wide(inner + rank * my_inner, my_inner),
        wide(2 * inner, channels - inner),
        piece(w_q, 0, qc),
        jnp.concatenate([pick(w, 0, HD, kv, heads) for w in (w_k, w_v)], 1).astype(BF),
        jnp.concatenate([dt, blank], 1).astype(BF),
        piece(w_out, 0, my_inner),
        piece(w_o, 0, qc),
    ]
    at = 0
    for part in parts:
        ab_ref[:, at : at + part.shape[1]] = part
        at += part.shape[1]
    for i, w in enumerate((w_gate, w_up, w_down)):
        cd_ref[:, i * my_hidden : (i + 1) * my_hidden] = piece(w, 0, my_hidden)


def reorder_kernel(back, count, at_ref, *refs):
    at = at_ref[0]
    for x_ref, o_ref in zip(refs[:count], refs[count:]):
        size = x_ref.shape[1] // 8
        for i, m in enumerate(ORDER):
            there = pl.ds(pl.multiple_of((at ^ m) * size, 128), size)
            here = pl.ds(i * size, size)
            if back:
                o_ref[:, there] = x_ref[:, here]
            else:
                o_ref[:, here] = x_ref[:, there]


def reorder(arrays, back=False):
    at = lax.axis_index("fsdp").astype(jnp.int32).reshape(1)
    vmem = pl.BlockSpec(memory_space=pltpu.VMEM)
    return pl.pallas_call(
        functools.partial(reorder_kernel, back, len(arrays)),
        out_shape=[jax.ShapeDtypeStruct(a.shape, a.dtype) for a in arrays],
        in_specs=[pl.BlockSpec(memory_space=pltpu.SMEM)] + [vmem] * len(arrays),
        out_specs=[vmem] * len(arrays),
    )(at, *arrays)


def lay_kernel(plan, n, kv_of, rank_ref, *refs):
    blocks, outs = refs[:n], refs[n:]
    rank = rank_ref[0]
    for kind, src, size, out, base in plan:
        o_ref = outs[out]
        if kind == "slice":
            for k in range(n):
                owner = lax.rem(rank - k + n, n)
                there = pl.ds(pl.multiple_of(base + owner * size, 128), size)
                o_ref[:, there] = blocks[k][:, src : src + size].astype(F32)
        elif kind == "sum":
            total = blocks[0][:, src : src + size].astype(F32)
            for k in range(1, n):
                total += blocks[k][:, src : src + size].astype(F32)
            o_ref[:, base : base + size] = total
        elif kind == "kv":
            heads = o_ref.shape[1] // size
            pieces = [jnp.zeros((o_ref.shape[0], size), F32)] * heads
            for k in range(n):
                owner = lax.rem(rank - k + n, n)
                value = blocks[k][:, src : src + size].astype(F32)
                for h in range(heads):
                    pieces[h] = pieces[h] + jnp.where(kv_of(owner) == h, value, 0.0)
            o_ref[...] = jnp.concatenate(pieces, 1)
        else:
            value = [blocks[k][:, src : src + size].astype(F32) for k in range(n)]
            for p in range(n):
                total = jnp.zeros_like(value[0])
                for k in range(n):
                    owner = lax.rem(rank - k + n, n)
                    total = jnp.where(owner == p, value[k], total)
                o_ref[:, base + p * size : base + (p + 1) * size] = total


def lay(blocks, plan, widths, kv_of):
    n = len(blocks)
    rank = lax.axis_index("dp").astype(jnp.int32).reshape(1)
    vmem = pl.BlockSpec(memory_space=pltpu.VMEM)
    return pl.pallas_call(
        functools.partial(lay_kernel, plan, n, kv_of),
        out_shape=[jax.ShapeDtypeStruct((blocks[0].shape[0], w), F32) for w in widths],
        in_specs=[pl.BlockSpec(memory_space=pltpu.SMEM)] + [vmem] * n,
        out_specs=[vmem] * len(widths),
    )(rank, *blocks)


def peer_send(blocks):
    n = lax.axis_size("dp")
    return [blocks[0]] + [
        lax.ppermute(blocks[k], "dp", [(i, (i - k) % n) for i in range(n)])
        for k in range(n - 1, 0, -1)
    ]


def peer_scalar_sum(v):
    n = lax.axis_size("dp")
    total = v
    for m in range(1, n):
        got = lax.ppermute(v, "dp", [(i, (i - m) % n) for i in range(n)])
        total = total + jnp.roll(got, -m, 0)
    return total


def sum_level(values):
    while len(values) > 1:
        values = [values[i] + values[i + 1] for i in range(0, len(values), 2)]
    return values[0]


def sum_dp(v):
    n = lax.axis_size("dp")
    return [v] + [
        lax.ppermute(v, "dp", [(i, i ^ m) for i in range(n)]) for m in range(1, n)
    ]


def sum_fsdp(v, step=1, stop=None):
    n = stop or lax.axis_size("fsdp")
    while step < n:
        v = v + lax.ppermute(v, "fsdp", [(i, i ^ step) for i in range(lax.axis_size("fsdp"))])
        step *= 2
    return v


def transposed(m):
    return jnp.swapaxes(m, 0, 1)


def column(row):
    size = row.shape[1]
    return transposed(jnp.broadcast_to(row, (size, size)))


def columns(ref):
    return jnp.concatenate([column(ref[k])[:, :1] for k in range(ref.shape[0])], 0)


def exact(a, b, dims):
    return lax.dot_general(a, b, (dims, ((), ())), precision=HIGH, preferred_element_type=F32)


def quick(a, b, dims):
    return lax.dot_general(
        a.astype(BF), b.astype(BF), (dims, ((), ())), preferred_element_type=F32
    )


NN, NT, TN = ((1,), (0,)), ((1,), (1,)), ((0,), (0,))


def shift_down(x, lag):
    return jnp.concatenate([jnp.zeros((lag, x.shape[1]), x.dtype), x[: x.shape[0] - lag]], 0)


def shift_up(x, lag):
    return jnp.concatenate([x[lag:], jnp.zeros((lag, x.shape[1]), x.dtype)], 0)


def branch_common(start, proj, conv_p, head_p, sizes):
    rows, inner, both, _ = sizes
    t_col = lax.broadcasted_iota(jnp.int32, (rows, rows), 0)
    s_row = lax.broadcasted_iota(jnp.int32, (rows, rows), 1)
    start_t = start.astype(F32)
    keep = (start_t == transposed(start_t)) & (s_row <= t_col)
    first = start_t[:, :1].astype(jnp.int32)
    t_one = t_col[:, :1]
    conv_in = proj[:, inner : 2 * inner + both]
    conv = conv_in * conv_p[3:4]
    lagged = []
    for lag in range(1, 4):
        ok = t_one - lag >= first
        moved = jnp.where(ok, shift_down(conv_in, lag), 0.0)
        lagged.append((ok, moved))
        conv = conv + moved * conv_p[3 - lag : 4 - lag]
    pre = conv + conv_p[4:5]
    gate = jax.nn.sigmoid(pre)
    act = pre * gate
    x, b, c = act[:, :inner], act[:, inner : inner + both // 2], act[:, inner + both // 2 :]
    dt = proj[:, proj.shape[1] - 128 :] + head_p[2:3]
    delta = jnp.maximum(dt, 0.0) + jnp.log1p(jnp.exp(-jnp.abs(dt)))
    decay_log = -delta * jnp.exp(head_p[0:1])
    lower = (s_row <= t_col).astype(F32)
    cum = exact(lower, decay_log, NN)
    cum_t, delta_t = transposed(cum), transposed(delta)
    scores = exact(c, b, NT)

    def head_decay(h):
        gap = cum[:, h : h + 1] - cum_t[h : h + 1]
        return jnp.where(keep, jnp.exp(jnp.where(keep, gap, 0.0)), 0.0)

    return dict(
        t_col=t_col, s_row=s_row, keep=keep, first=first, t_one=t_one, conv_in=conv_in,
        lagged=lagged, pre=pre, gate=gate, x=x, b=b, c=c, dt=dt, delta=delta,
        decay_log=decay_log, lower=lower, delta_t=delta_t, scores=scores, head_decay=head_decay,
    )


def swap_halves(x):
    lane = lax.broadcasted_iota(jnp.int32, x.shape, 1)
    size, half = x.shape[1], HD // 2
    low = lane % HD < half
    return jnp.where(low, pltpu.roll(x, size - half, 1), pltpu.roll(x, half, 1))


def rotary(first, rows):
    lane = lax.broadcasted_iota(jnp.int32, (rows, 128), 1)
    t = lax.broadcasted_iota(jnp.int32, (rows, 128), 0)
    half = HD // 2
    frequency = jnp.exp((lane % half).astype(F32) * (-2.0 / HD * math.log(rope_base)))
    angle = (t - first).astype(F32) * frequency
    return jnp.cos(angle), jnp.where(lane % HD < half, -jnp.sin(angle), jnp.sin(angle))


def attn_common(q, kv, first, keep):
    rows = q.shape[0]
    lane = lax.broadcasted_iota(jnp.int32, (rows, 128), 1)
    low = lane < HD
    cosine, sine = rotary(first, rows)
    q_rot = q * cosine + swap_halves(q) * sine
    k_rot = kv * cosine + swap_halves(kv) * sine
    keys = jnp.where(low, k_rot, pltpu.roll(k_rot, HD, 1))
    values = jnp.where(low, pltpu.roll(kv, HD, 1), kv)
    probs, picks = [], []
    for h in range(2):
        pick = low if h == 0 else ~low
        logits = exact(jnp.where(pick, q_rot, 0.0), keys, NT) * HD ** (-0.5)
        logits = jnp.where(keep, logits, -1e30)
        expo = jnp.exp(logits - jnp.max(logits, -1, keepdims=True))
        probs.append(expo / jnp.sum(expo, -1, keepdims=True))
        picks.append(pick)
    return low, cosine, sine, q_rot, keys, values, probs, picks


def branch_forward(
    sizes, n, *refs
):
    a0_ref, a1_ref, g_ref, conv_ref, head_ref = refs[n : n + 5]
    normed_ref, proj_ref, y_ref, gated_ref, square_ref, x_ref = refs[n + 5 :]
    for k in range(n):

        @pl.when(pl.program_id(0) == k)
        def _():
            x_ref[...] = refs[k][...]

    rows, inner, _, heads = sizes
    width = g_ref.shape[1]
    x32 = x_ref[:, :width].astype(F32)
    scale = lax.rsqrt(jnp.mean(x32 * x32, -1, keepdims=True) + norm_eps)
    normed = (x32 * scale * g_ref[...]).astype(BF)
    normed_ref[...] = normed
    half = a0_ref.shape[0]
    proj = mm(normed[:, :half], a0_ref[...]) + mm(normed[:, half:], a1_ref[...])
    proj_ref[...] = proj
    start = x_ref[:, width:]
    conv_p, head_p = conv_ref[...], head_ref[...]
    v = branch_common(start, proj, conv_p, head_p, sizes)
    low = v["s_row"] < HD
    outs = []
    for pair in range(heads // 2):
        x_pair = v["x"][:, pair * 128 : pair * 128 + 128]
        y = []
        for h in (2 * pair, 2 * pair + 1):
            mixer = v["scores"] * v["head_decay"](h) * v["delta_t"][h : h + 1]
            y.append(quick(mixer, x_pair, NN))
        outs.append(jnp.where(low, y[0], y[1]))
    y = jnp.concatenate(outs, 1) + conv_p[5:6, :inner] * v["x"]
    z = proj[:, :inner]
    gated = y * (z * jax.nn.sigmoid(z))
    y_ref[...] = y
    gated_ref[...] = gated
    square = jnp.sum(gated * gated, -1, keepdims=True)
    square_ref[0] = transposed(jnp.broadcast_to(square, (rows, rows)))[:1]


def links(start):
    shape = start.shape
    t_col = lax.broadcasted_iota(jnp.int32, shape, 0)
    s_row = lax.broadcasted_iota(jnp.int32, shape, 1)
    return start[:, :1].astype(jnp.int32), (start == transposed(start)) & (s_row <= t_col)


def attn_forward(x_ref, qkv_ref, attn_ref):
    first, keep = links(x_ref[...].astype(F32))
    low, _, _, _, _, values, probs, _ = attn_common(
        qkv_ref[:, :128], qkv_ref[:, 128:], first, keep
    )
    out = [quick(p, values, NN) for p in probs]
    attn_ref[...] = jnp.where(low, out[0], out[1]).astype(BF)


def branch_back_out(
    inner, low, n, *refs
):
    b0_ref, b1_ref, gated_ref, scale_ref, gm_ref = refs[n : n + 5]
    d_scaled_ref, d_attn_ref, inner_ref, g_gm_ref, dm_ref = refs[n + 5 :]
    dm = jnp.concatenate([r[...] for r in refs[:n]], 0)
    dm_ref[...] = dm
    d_mix = halved(dm, b0_ref[:, low:], b1_ref[:, low:])
    d_out = d_mix[:, :inner]
    gated = gated_ref[...]
    g_gm_ref[...] = jnp.sum(d_out * gated * columns(scale_ref), 0, keepdims=True)
    d_scaled = d_out * gm_ref[...]
    d_scaled_ref[...] = d_scaled
    dot = jnp.sum(d_scaled * gated, -1, keepdims=True)
    rows = inner_ref.shape[2]
    for k in range(inner_ref.shape[0]):
        block = jnp.broadcast_to(dot[k * rows : (k + 1) * rows], (rows, rows))
        inner_ref[k] = transposed(block)[:1]
    d_attn_ref[...] = d_mix[:, inner:]


def branch_back_attn(x_ref, qkv_ref, d_attn_ref, d_qkv_ref):
    start = x_ref[...].astype(F32)
    rows = start.shape[0]
    first, keep = links(start)
    q, kv = qkv_ref[:, :128], qkv_ref[:, 128:]
    low, cosine, sine, q_rot, keys, values, probs, picks = attn_common(q, kv, first, keep)
    d_attn = d_attn_ref[...]
    d_q = []
    d_k = jnp.zeros((rows, 128), F32)
    d_v = jnp.zeros((rows, 128), F32)
    for p, pick in zip(probs, picks):
        d_head = jnp.where(pick, d_attn, 0.0)
        d_p = quick(d_head, values, NT)
        d_logit = p * (d_p - jnp.sum(d_p * p, -1, keepdims=True)) * HD ** (-0.5)
        d_q.append(quick(d_logit, keys, NN))
        d_k += quick(d_logit, jnp.where(pick, q_rot, 0.0), TN)
        d_v += quick(p, d_head, TN)
    d_q = jnp.where(low, d_q[0], d_q[1])
    d_k = d_k + pltpu.roll(d_k, HD, 1)
    d_v = d_v + pltpu.roll(d_v, HD, 1)
    d_q = d_q * cosine + swap_halves(d_q * sine)
    d_k = d_k * cosine + swap_halves(d_k * sine)
    d_qkv_ref[:, :128] = d_q.astype(BF)
    d_qkv_ref[:, 128:] = jnp.where(low, d_k, d_v).astype(BF)


def branch_back_mamba(
    sizes, q_at, x_ref, proj_ref, y_ref, gated_ref, d_scaled_ref, scale_ref, inner_ref,
    d_qkv_ref, conv_ref, head_ref, whole,
    d_proj_ref, g_conv_ref, g_head_ref, g_skip_ref,
):
    rows, inner, both, heads = sizes

    @pl.when(pl.program_id(0) == 0)
    def _():
        g_conv_ref[...] = jnp.zeros_like(g_conv_ref)
        g_head_ref[...] = jnp.zeros_like(g_head_ref)
        g_skip_ref[...] = jnp.zeros_like(g_skip_ref)

    proj = proj_ref[...]
    conv_p, head_p = conv_ref[...], head_ref[...]
    v = branch_common(x_ref[...], proj, conv_p, head_p, sizes)
    scale = column(scale_ref[0])[:, :1]
    dot = column(inner_ref[0])[:, :1]
    d_gated = scale * d_scaled_ref[...] - gated_ref[...] * (scale * scale * scale * dot / whole)
    z = proj[:, :inner]
    zs = jax.nn.sigmoid(z)
    d_y = d_gated * (z * zs)
    d_z = d_gated * y_ref[...] * (zs * (1.0 + z * (1.0 - zs)))
    d_proj_ref[:, :inner] = d_z.astype(BF)
    x, scores, delta_t = v["x"], v["scores"], v["delta_t"]
    g_skip_ref[...] += jnp.sum(d_y * x, 0, keepdims=True)
    low = v["s_row"] < HD
    d_x = []
    d_scores = jnp.zeros((rows, rows), F32)
    d_cum = jnp.zeros((rows, rows), F32)
    d_delta_rows, d_cum_rows = [], []
    for pair in range(heads // 2):
        at = slice(pair * 128, pair * 128 + 128)
        x_pair, dy_pair = x[:, at], d_y[:, at]
        parts = []
        for h in (2 * pair, 2 * pair + 1):
            pick = low if h % 2 == 0 else ~low
            decay = v["head_decay"](h)
            scored = scores * decay
            mixer = scored * delta_t[h : h + 1]
            d_mixer = quick(jnp.where(pick, dy_pair, 0.0), x_pair, NT)
            parts.append(quick(mixer, dy_pair, TN))
            d_scores += d_mixer * (decay * delta_t[h : h + 1])
            d_delta_rows.append(jnp.sum(d_mixer * scored, 0, keepdims=True))
            flow = d_mixer * mixer
            d_cum_rows.append(jnp.sum(flow, 0, keepdims=True))
            d_cum = jnp.where(v["s_row"] == h, jnp.sum(flow, -1, keepdims=True), d_cum)
        d_x.append(jnp.where(low, parts[0], parts[1]))
    blank = jnp.zeros((rows - heads, rows), F32)
    d_delta = transposed(jnp.concatenate(d_delta_rows + [blank], 0))
    d_cum = d_cum - transposed(jnp.concatenate(d_cum_rows + [blank], 0))
    d_log = exact(v["lower"], d_cum, TN)
    d_delta = d_delta - jnp.exp(head_p[0:1]) * d_log
    d_dt = d_delta * jax.nn.sigmoid(v["dt"])
    g_head_ref[0:1] += jnp.sum(d_log * v["decay_log"], 0, keepdims=True)
    g_head_ref[1:2] += jnp.sum(d_dt, 0, keepdims=True)
    d_proj_ref[:, d_proj_ref.shape[1] - 128 :] = d_dt.astype(BF)
    d_act = jnp.concatenate(
        d_x + [quick(d_scores, v["c"], TN), quick(d_scores, v["b"], NN)], 1
    )
    d_act = jnp.concatenate(
        [d_act[:, :inner] + conv_p[5:6, :inner] * d_y, d_act[:, inner:]], 1
    )
    gate = v["gate"]
    d_conv = d_act * (gate * (1.0 + v["pre"] * (1.0 - gate)))
    g_conv_ref[4:5] += jnp.sum(d_conv, 0, keepdims=True)
    g_conv_ref[3:4] += jnp.sum(d_conv * v["conv_in"], 0, keepdims=True)
    d_in = d_conv * conv_p[3:4]
    for lag, (ok, moved) in zip(range(1, 4), v["lagged"]):
        g_conv_ref[3 - lag : 4 - lag] += jnp.sum(d_conv * moved, 0, keepdims=True)
        back = shift_up(jnp.where(ok, d_conv, 0.0), lag)
        d_in = d_in + back * conv_p[3 - lag : 4 - lag]
    d_proj_ref[:, inner : 2 * inner + both] = d_in.astype(BF)
    d_proj_ref[:, q_at : q_at + 256] = d_qkv_ref[...]


def halved(left, w0, w1):
    half = w0.shape[0]
    return mm(left[:, :half], w0) + mm(left[:, half:], w1)


def put_rows(outs, left, w0, w1):
    value = jnp.concatenate([mul_t(left, w0), mul_t(left, w1)], 1)
    rows = left.shape[0] // len(outs)
    for k, o_ref in enumerate(outs):
        o_ref[...] = value[k * rows : (k + 1) * rows].astype(o_ref.dtype)
    return value


def rows_out(n, rows, width):
    return [out_of((rows, width), F32)] + [out_of((rows, width), BF)] * (n - 1)


def rows_kernel(low, high, left_ref, w0_ref, w1_ref, *outs):
    put_rows(outs, left_ref[...], w0_ref[:, low:high], w1_ref[:, low:high])


def back_in_kernel(width, span, left_ref, x_ref, w0_ref, w1_ref, g_in_ref, *outs):
    value = put_rows(outs, left_ref[...], w0_ref[:, :span], w1_ref[:, :span])
    x32 = x_ref[:, :width].astype(F32)
    scale = lax.rsqrt(jnp.mean(x32 * x32, -1, keepdims=True) + norm_eps)
    g_in_ref[...] = jnp.sum(value * x32 * scale, 0, keepdims=True)


def partial_rows(n, left, halves, low, high):
    rows, width = left.shape[0] // n, 2 * halves[0].shape[0]
    return pl.pallas_call(
        functools.partial(rows_kernel, low, high), out_shape=rows_out(n, rows, width)
    )(left, *halves)


def mix_kernel(low, gated_ref, scale_ref, gm_ref, attn_ref, w0_ref, w1_ref, mix_ref, *outs):
    scale = columns(scale_ref)
    mamba = (gated_ref[...] * scale * gm_ref[...]).astype(BF)
    mix = jnp.concatenate([mamba, attn_ref[...]], 1)
    mix_ref[...] = mix
    put_rows(outs, mix, w0_ref[:, low:], w1_ref[:, low:])


def ffn_kernel(size, n, *refs):
    cot_ref, w0_ref, w1_ref, act_ref, d_gu_ref, hid_ref, *outs = refs[n:]
    hid = jnp.concatenate([r[...] for r in refs[:n]], 0)
    hid_ref[...] = hid
    gu = halved(hid, w0_ref[:, : 2 * size], w1_ref[:, : 2 * size])
    gate, up = gu[:, :size], gu[:, size:]
    sig = jax.nn.sigmoid(gate)
    silu = gate * sig
    act_ref[...] = (silu * up).astype(BF)
    d_act = halved(cot_ref[...], w0_ref[:, 2 * size :], w1_ref[:, 2 * size :])
    d_gate = d_act * up * (sig * (1.0 + gate * (1.0 - sig)))
    d_gu = jnp.concatenate([d_gate.astype(BF), (d_act * silu).astype(BF)], 1)
    d_gu_ref[...] = d_gu
    put_rows(outs, d_gu, w0_ref[:, : 2 * size], w1_ref[:, : 2 * size])


def row_spec(*shape):
    return pl.BlockSpec(shape, lambda i: (i,) + (0,) * (len(shape) - 1))


def fixed_spec(a):
    return pl.BlockSpec(a.shape, lambda i: (0,) * len(a.shape))


def out_of(shape, dtype):
    return jax.ShapeDtypeStruct(shape, dtype)


def rms_scale(x):
    return lax.rsqrt(jnp.mean(x * x, -1, keepdims=True) + norm_eps)


def rms_back(x, scale, gain, d_out):
    scaled = d_out * gain
    inner = jnp.mean(scaled * x, -1, keepdims=True)
    return scale * scaled - x * (scale * scale * scale * inner), jnp.sum(d_out * x * scale, 0)


def body(
    tokens,
    segment_ids,
    cotangent,
    w_in,
    w_q,
    w_k,
    w_v,
    w_o,
    w_out,
    w_gate,
    w_up,
    w_down,
    g_in,
    g_ff,
    g_mamba,
    conv_weight,
    conv_bias,
    a_log,
    d_skip,
    dt_bias,
):
    n = lax.axis_size("dp")
    rank = lax.axis_index("dp")
    rows, width = tokens.shape
    inner, channels, heads = g_mamba.shape[0], conv_bias.shape[0], a_log.shape[0]
    hidden = w_gate.shape[1]
    q_heads, kv_heads = w_q.shape[1] // HD, w_k.shape[1] // HD
    my_inner, my_heads, my_hidden, my_q = inner // n, heads // n, hidden // n, q_heads // n
    per_kv = q_heads // kv_heads
    assert heads % n == 0 and q_heads % n == 0 and hidden % n == 0 and per_kv % my_q == 0
    both = channels - inner
    qc = my_q * HD

    cube = is_cube(width)
    tail_pad = -my_heads % 128
    assert rows <= 256
    start = (segment_ids - segment_ids[0]).astype(BF)
    start = jnp.broadcast_to(start[:, None], (rows, 128))
    o = 2 * my_inner + both
    span = o + qc + 2 * HD + my_heads + tail_pad
    mc = my_inner + qc
    vmem = pl.BlockSpec(memory_space=pltpu.VMEM)
    shards = (w_in.T, w_q, w_k, w_v, w_o, w_out, w_gate, w_up, w_down)
    dims = (inner, channels, my_inner, my_heads, my_hidden, qc, my_q, per_kv, n)
    sh_a, sh_b = pl.pallas_call(
        functools.partial(slice_kernel, dims),
        out_shape=[
            out_of((w_in.shape[0], span + mc), BF),
            out_of((w_in.shape[0], 3 * my_hidden), BF),
        ],
        in_specs=[pl.BlockSpec(memory_space=pltpu.SMEM)] + [vmem] * 9,
        out_specs=[vmem] * 2,
    )(rank.astype(jnp.int32).reshape(1), *shards)
    if cube:
        parts_a = gather_start(sh_a)
        tokens, cotangent, g_in, g_ff = reorder(
            [tokens, cotangent, g_in.reshape(1, width), g_ff.reshape(1, width)]
        )
    first = peer_blocks(jnp.concatenate([tokens, start], 1))
    if cube:
        parts_a, tok_held = tie((parts_a, first[-2]))
        own_a = jnp.concatenate(parts_a, 0)
        halves_a = [own_a, flip(own_a, 1)]
        tok_blocks, first = first, jnp.concatenate(first, 0)
    else:
        tok_held = first[-2]
        tok_blocks, first = first, jnp.concatenate(first, 0)
        full_a = lax.all_gather(sh_a, "fsdp", axis=0, tiled=True)
        halves_a = [full_a[: width // 2], full_a[width // 2 :]]

    if cube:
        sh_b, parts_a = tie((sh_b, parts_a))
        parts_b = gather_start(sh_b)
    cot_first, _ = tie((cotangent, tok_held))
    cot_blocks = peer_direct(cot_first)

    assert n == 4 and lax.axis_size("fsdp") & (lax.axis_size("fsdp") - 1) == 0
    assert rows == 128 and qc == 128 and 2 * HD == 128 and conv_weight.shape[0] == 4
    assert my_heads % 2 == 0 and both % 256 == 0 and inner // heads == HD
    assert o % 256 == 0 and width % 128 == 0
    cw = jnp.concatenate(
        [cols(conv_weight, rank * my_inner, my_inner), conv_weight[:, inner:]], 1
    )
    cb = jnp.concatenate(
        [lax.dynamic_slice(conv_bias, (rank * my_inner,), (my_inner,)), conv_bias[inner:]]
    )

    def mine(p, size):
        return lax.dynamic_slice(p, (rank * size,), (size,))

    gm = mine(g_mamba, my_inner)

    sizes = (rows, my_inner, both, my_heads)
    skip = jnp.repeat(mine(d_skip, my_heads), HD)
    conv_p = jnp.concatenate(
        [cw, cb[None], jnp.pad(skip, (0, both))[None], jnp.zeros((2, cw.shape[1]), F32)], 0
    )
    head_p = jnp.stack(
        [mine(a_log, my_heads), mine(d_skip, my_heads), mine(dt_bias, my_heads)], 0
    )
    head_p = jnp.pad(head_p, ((0, 5), (0, 128 - my_heads)))
    gm = gm.reshape(1, my_inner)
    g_in_row = g_in.reshape(1, width)
    count = n * rows
    normed, proj, y, gated, square = pl.pallas_call(
        functools.partial(branch_forward, sizes, n),
        grid=(n,),
        scratch_shapes=[pltpu.VMEM((rows, first.shape[1]), BF)],
        in_specs=[fixed_spec(a) for a in tok_blocks]
        + [pl.BlockSpec((a.shape[0], span), lambda i: (0, 0)) for a in halves_a]
        + [fixed_spec(a) for a in (g_in_row, conv_p, head_p)],
        out_specs=[
            row_spec(rows, width),
            row_spec(rows, span),
            row_spec(rows, my_inner),
            row_spec(rows, my_inner),
            row_spec(1, 1, rows),
        ],
        out_shape=[
            out_of((count, width), BF),
            out_of((count, span), F32),
            out_of((count, my_inner), F32),
            out_of((count, my_inner), F32),
            out_of((n, 1, rows), F32),
        ],
    )(*tok_blocks, *halves_a, g_in_row, conv_p, head_p)
    square = peer_scalar_sum(square.reshape(n, rows))
    start_spec = pl.BlockSpec((rows, 128), lambda i: (i, width // 128))
    qkv_spec = pl.BlockSpec((rows, 256), lambda i: (i, o // 256))
    attn = pl.pallas_call(
        attn_forward,
        grid=(n,),
        in_specs=[start_spec, qkv_spec],
        out_specs=row_spec(rows, qc),
        out_shape=out_of((count, qc), BF),
    )(first, proj)
    scale_rows = lax.rsqrt(square / inner + norm_eps).reshape(n, 1, rows)
    shapes = rows_out(n, rows, width)
    mix_in, *mix_parts = pl.pallas_call(
        functools.partial(mix_kernel, span),
        out_shape=[out_of((count, mc), BF)] + shapes,
    )(gated, scale_rows, gm, attn, *halves_a)
    mix_parts = peer_send(mix_parts)
    if cube:
        mix_parts, cot_blocks = tie((mix_parts, cot_blocks))
        own_b = jnp.concatenate(parts_b, 0)
        halves_b = [own_b, flip(own_b, 1)]
    else:
        full_b = lax.all_gather(sh_b, "fsdp", axis=0, tiled=True)
        halves_b = [full_b[: width // 2], full_b[width // 2 :]]
    cot_all = jnp.concatenate(cot_blocks, 0)
    tok32 = tokens.astype(F32)
    mixed = tok32 + add_up(mix_parts)
    f_scale = rms_scale(mixed)
    hid_blocks = peer_blocks((mixed * f_scale * g_ff).astype(BF))
    act, d_gu, hid_all, *d_hidden = pl.pallas_call(
        functools.partial(ffn_kernel, my_hidden, n),
        out_shape=[out_of((count, my_hidden), BF), out_of((count, 2 * my_hidden), BF)]
        + [out_of((count, width), BF)]
        + shapes,
    )(*hid_blocks, cot_all, *halves_b)
    d_hidden = peer_send(d_hidden)
    c_pairs = [(hid_all, d_gu), (cot_all, act)]
    if cube:
        c_own = scatter_own(c_pairs, scatter_first(c_pairs))
        grad_c = scatter_rest(c_own)
        d_hidden, c_own = tie((d_hidden, c_own))
    else:
        grad_c = grads(c_pairs, 0, width)
    d_mixed_n, grad_g_ff = rms_back(mixed, f_scale, g_ff, add_up(d_hidden))
    d_mixed = cotangent.astype(F32) + d_mixed_n
    dm_blocks = peer_blocks(d_mixed.astype(BF))
    dm_blocks, grad_c = tie((dm_blocks, grad_c))
    if cube:
        grad_c = add_up(grad_c).astype(BF)
    else:
        grad_c = lax.psum_scatter(grad_c, "fsdp", scatter_dimension=0, tiled=True)
    c_blocks = peer_direct(grad_c)
    out_parts = partial_rows(n, act, halves_b, 2 * my_hidden, 3 * my_hidden)
    out_parts = peer_send(out_parts)
    d_scaled, d_attn, m_inner, grad_gm, dm_all = pl.pallas_call(
        functools.partial(branch_back_out, my_inner, span, n),
        out_shape=[
            out_of((count, my_inner), F32),
            out_of((count, qc), F32),
            out_of((n, 1, rows), F32),
            out_of((1, my_inner), F32),
            out_of((count, width), BF),
        ],
    )(*dm_blocks, *halves_a, gated, scale_rows, gm)
    d_qkv = pl.pallas_call(
        branch_back_attn,
        grid=(n,),
        in_specs=[start_spec, qkv_spec, row_spec(rows, qc)],
        out_specs=row_spec(rows, 256),
        out_shape=out_of((count, 256), BF),
        cost_estimate=pl.CostEstimate(
            flops=30 * count * rows * 128, bytes_accessed=count * 5000, transcendentals=count * 512
        ),
    )(first, proj, d_attn)
    m_inner = peer_scalar_sum(m_inner.reshape(n, rows)).reshape(n, 1, rows)
    m_inner, d_qkv = tie((m_inner, d_qkv))
    d_proj, g_conv, g_head, g_skip = pl.pallas_call(
        lambda *refs: branch_back_mamba(sizes, o, *refs[:10], float(inner), *refs[10:]),
        grid=(n,),
        in_specs=[
            start_spec,
            row_spec(rows, span),
            row_spec(rows, my_inner),
            row_spec(rows, my_inner),
            row_spec(rows, my_inner),
            row_spec(1, 1, rows),
            row_spec(1, 1, rows),
            row_spec(rows, 256),
            fixed_spec(conv_p),
            fixed_spec(head_p),
        ],
        out_specs=[
            row_spec(rows, span),
            fixed_spec(conv_p),
            fixed_spec(head_p),
            fixed_spec(gm),
        ],
        out_shape=[
            out_of((count, span), BF),
            out_of(conv_p.shape, F32),
            out_of(head_p.shape, F32),
            out_of((1, my_inner), F32),
        ],
    )(first, proj, y, gated, d_scaled, scale_rows, m_inner, d_qkv, conv_p, head_p)
    a_pairs = [(dm_all, mix_in), (normed, d_proj)]
    if cube:
        got = scatter_first(a_pairs)
        d_proj, _ = tie((d_proj, a_pairs))
    grad_g_in, *d_normed = pl.pallas_call(
        functools.partial(back_in_kernel, width, span),
        out_shape=[out_of((1, width), F32)] + shapes,
    )(d_proj, first, *halves_a)

    def place(v):
        spot = (jnp.arange(n) == rank).astype(F32)
        spread = spot[:, None, None] * v.reshape(v.shape[:-1] + (1, -1, 128))
        return spread.reshape(-1, 128)

    def ordered(v):
        v = v.reshape(-1, 128)
        if not cube:
            return v
        block = jnp.array(ORDER) ^ lax.axis_index("fsdp")
        hit = (jnp.arange(8)[:, None] == block[None, :]).astype(F32)
        v = v.reshape(8, 1, -1)
        return jnp.sum(hit.T[:, :, None] * v, 0).reshape(-1, 128)

    def head_row(v):
        spot = (jnp.arange(n) == rank).astype(F32)
        return jnp.pad((spot[:, None] * v[None]).reshape(1, -1), ((0, 0), (0, 128 - heads)))

    grad_gm, g_cw, g_cb = grad_gm[0], g_conv[:4], g_conv[4]
    g_al, g_db = g_head[0, :my_heads], g_head[1, :my_heads]
    g_ds = jnp.sum(g_skip.reshape(my_heads, HD), 1)
    small = [ordered(grad_g_in), ordered(grad_g_ff), place(grad_gm)]
    for row in range(g_cw.shape[0]):
        small += [place(g_cw[row, :my_inner]), g_cw[row, my_inner:].reshape(-1, 128)]
    small += [place(g_cb[:my_inner]), g_cb[my_inner:].reshape(-1, 128)]
    small += [head_row(g_al), head_row(g_ds), head_row(g_db)]
    flat = jnp.concatenate(small)
    flat = jnp.pad(flat, ((0, -flat.shape[0] % 8), (0, 0)))
    flat = sum_dp(flat)

    if cube:
        own = scatter_own(a_pairs, got)
        grad_a = scatter_rest(own)
        d_normed, c_blocks, out_parts, own = tie((d_normed, c_blocks, out_parts, own))
        d_normed = peer_send(d_normed)
        grad_a = add_up(grad_a).astype(BF)
    else:
        d_normed = peer_send(d_normed)
        grad_a = lax.psum_scatter(
            grads(a_pairs, 0, width), "fsdp", scatter_dimension=0, tiled=True
        )
    output = (mixed + add_up(out_parts)).astype(BF)
    d_tok_n, _ = rms_back(tok32, rms_scale(tok32), g_in, add_up(d_normed))
    grad_tokens = (d_mixed + d_tok_n).astype(BF)
    if cube:
        output, grad_tokens = reorder([output, grad_tokens], back=True)

    a_blocks = [grad_a, next_peer(grad_a)]
    while len(a_blocks) < n:
        a_blocks[-1], flat = tie((a_blocks[-1], flat))
        a_blocks.append(next_peer(a_blocks[-1]))
        if len(a_blocks) == 3:
            flat = sum_fsdp(sum_level(flat), 1, 4)
    flat = sum_fsdp(flat, 4)

    def kv_of(owner):
        return owner * my_q // per_kv

    grad_gate, grad_up, grad_down = lay(
        c_blocks,
        [("slice", i * my_hidden, my_hidden, i, 0) for i in range(3)],
        [hidden] * 3,
        kv_of,
    )
    grad_in, grad_q, grad_k, grad_v, grad_out, grad_o = lay(
        a_blocks,
        [
            ("slice", 0, my_inner, 4, 0),
            ("slice", my_inner, qc, 5, 0),
            ("slice", mc, my_inner, 0, 0),
            ("slice", mc + my_inner, my_inner, 0, inner),
            ("sum", mc + 2 * my_inner, both, 0, 2 * inner),
            ("slice", mc + o, qc, 1, 0),
            ("kv", mc + o + qc, HD, 2, 0),
            ("kv", mc + o + qc + HD, HD, 3, 0),
            ("tail", mc + o + qc + 2 * HD, my_heads, 0, inner + channels),
        ],
        [w_in.shape[1], w_q.shape[1], w_k.shape[1], w_v.shape[1], inner, w_o.shape[1]],
        kv_of,
    )

    sizes = [width, width, inner, g_cw.shape[0] * channels, channels]
    sums, at = [], 0
    for size in sizes:
        sums.append(flat[at : at + size // 128].reshape(-1))
        at += size // 128
    for i in range(3):
        sums.append(flat[at + i, :heads])
    return (
        output,
        grad_tokens,
        grad_in,
        grad_q,
        grad_k,
        grad_v,
        grad_o,
        grad_out,
        grad_gate,
        grad_up,
        grad_down,
        sums[0],
        sums[1],
        sums[2],
        sums[3].reshape(conv_weight.shape),
        sums[4],
        sums[5],
        sums[6],
        sums[7],
    )


def solution(mesh):
    rows, shard, whole = P(("fsdp", "dp"), None), P("fsdp", None), P()
    in_specs = (rows, P(("fsdp", "dp")), rows) + (shard,) * 9 + (whole,) * 8
    out_specs = (rows, rows) + (shard,) * 9 + (whole,) * 8

    return jax.shard_map(body, mesh=mesh, in_specs=in_specs, out_specs=out_specs, check_vma=False)
```

```python
import functools
import math

import jax
import jax.numpy as jnp
from jax import lax
from jax.experimental import pallas as pl
from jax.experimental.pallas import tpu as pltpu
from jax.sharding import PartitionSpec as P


HD = 64
norm_eps = 1e-05
rope_base = 10000.0
HIGH = lax.Precision.HIGHEST
BF = jnp.bfloat16
F32 = jnp.float32


def mm(left, right):
    return jnp.dot(left, right, preferred_element_type=F32)


def mul_t(left, right):
    return lax.dot_general(left, right, (((1,), (1,)), ((), ())), preferred_element_type=F32)


def t_mul(left, right):
    return lax.dot_general(left, right, (((0,), (0,)), ((), ())), preferred_element_type=F32)


def cols(w, start, size):
    return lax.dynamic_slice(w, (0, start), (w.shape[0], size))


tie = lax.optimization_barrier


def next_peer(x):
    n = lax.axis_size("dp")
    return lax.ppermute(x, "dp", [(i, (i + 1) % n) for i in range(n)])


def peer_blocks(x):
    blocks = [x]
    for _ in range(lax.axis_size("dp") - 1):
        blocks.append(next_peer(blocks[-1]))
    return blocks


def peer_direct(x):
    n = lax.axis_size("dp")
    return [x] + [
        lax.ppermute(x, "dp", [(i, (i + k) % n) for i in range(n)]) for k in range(n - 1, 0, -1)
    ][::-1]


def flip(x, bits):
    size = lax.axis_size("fsdp")
    return lax.ppermute(x, "fsdp", [(i, i ^ bits) for i in range(size)])


def is_cube(width):
    return lax.axis_size("fsdp") == 8 and width % 1024 == 0


ORDER = (0, 2, 4, 6, 1, 3, 5, 7)


def gather_start(w):
    return [w] + [flip(w, m) for m in ORDER[1:4]]


def scatter_first(pairs):
    height = pairs[0][0].shape[1]
    return flip(grads(pairs, height // 2, height), 1)


def scatter_own(pairs, got):
    return grads(pairs, 0, pairs[0][0].shape[1] // 2, add=got, blocks=4)


def scatter_rest(own):
    return [own[0]] + [flip(own[i], ORDER[i]) for i in range(1, 4)]


def add_up(parts):
    total = parts[0].astype(F32)
    for p in parts[1:]:
        total = total + p.astype(F32)
    return total


def grad_kernel(count, add, blocks, *refs):
    total = []
    for left, right in zip(refs[:count], refs[count : 2 * count]):
        total.append(t_mul(left[...], right[...]))
    total = jnp.concatenate(total, 1)
    outs = refs[2 * count :]
    if add:
        total = total + outs[0][...].astype(F32)
        outs = outs[1:]
    total = total.astype(BF)
    rows = total.shape[0] // blocks
    for i in range(blocks):
        outs[i][...] = total[i * rows : (i + 1) * rows]


def grads(pairs, low, high, add=None, blocks=1):
    depth = pairs[0][0].shape[0]
    height = high - low
    width = sum(r.shape[1] for _, r in pairs)
    rows = height // blocks
    out_shape = [jax.ShapeDtypeStruct((rows, width), BF)] * blocks
    out_specs = [pl.BlockSpec((rows, width), lambda i: (0, 0))] * blocks
    out = pl.pallas_call(
        functools.partial(grad_kernel, len(pairs), add is not None, blocks),
        out_shape=out_shape,
        grid=(1,),
        in_specs=[pl.BlockSpec((depth, height), lambda i: (0, low // height))] * len(pairs)
        + [pl.BlockSpec((depth, r.shape[1]), lambda i: (0, 0)) for _, r in pairs]
        + ([] if add is None else [pl.BlockSpec((height, width), lambda i: (0, 0))]),
        out_specs=out_specs,
        cost_estimate=pl.CostEstimate(
            flops=2 * depth * height * width,
            bytes_accessed=2 * (depth * (height * len(pairs) + width) + height * width),
            transcendentals=0,
        ),
    )(*[l for l, _ in pairs], *[r for _, r in pairs], *([] if add is None else [add]))
    return out[0] if blocks == 1 else out


def slice_kernel(dims, rank_ref, *refs):
    inner, channels, my_inner, my_heads, my_hidden, qc, my_q, per_kv, n = dims
    w_in, w_q, w_k, w_v, w_o, w_out, w_gate, w_up, w_down, ab_ref, cd_ref = refs
    rank = rank_ref[0]
    kv = rank * my_q // per_kv

    def wide(base, size):
        return jnp.swapaxes(w_in[pl.ds(pl.multiple_of(base, 128), size), :], 0, 1)

    def piece(ref, base, size):
        return ref[:, pl.ds(pl.multiple_of(base + rank * size, 128), size)]

    def pick(ref, base, size, which, count):
        value = ref[:, base : base + size].astype(F32)
        for i in range(1, count):
            at = base + i * size
            value = jnp.where(which == i, ref[:, at : at + size].astype(F32), value)
        return value

    heads = w_k.shape[1] // HD
    dt_at = inner + channels
    tail = w_in[dt_at : dt_at + n * my_heads, :].astype(F32)
    tail = jnp.concatenate([tail, jnp.zeros((128 - n * my_heads, tail.shape[1]), F32)], 0)
    tail = jnp.swapaxes(tail, 0, 1)
    dt = tail[:, :my_heads]
    for i in range(1, n):
        dt = jnp.where(rank == i, tail[:, i * my_heads : (i + 1) * my_heads], dt)
    blank = jnp.zeros((dt.shape[0], -my_heads % 128), F32)
    parts = [
        wide(rank * my_inner, my_inner),
        wide(inner + rank * my_inner, my_inner),
        wide(2 * inner, channels - inner),
        piece(w_q, 0, qc),
        jnp.concatenate([pick(w, 0, HD, kv, heads) for w in (w_k, w_v)], 1).astype(BF),
        jnp.concatenate([dt, blank], 1).astype(BF),
        piece(w_out, 0, my_inner),
        piece(w_o, 0, qc),
    ]
    at = 0
    for part in parts:
        ab_ref[:, at : at + part.shape[1]] = part
        at += part.shape[1]
    for i, w in enumerate((w_gate, w_up, w_down)):
        cd_ref[:, i * my_hidden : (i + 1) * my_hidden] = piece(w, 0, my_hidden)


def reorder_kernel(back, count, at_ref, *refs):
    at = at_ref[0]
    for x_ref, o_ref in zip(refs[:count], refs[count:]):
        size = x_ref.shape[1] // 8
        for i, m in enumerate(ORDER):
            there = pl.ds(pl.multiple_of((at ^ m) * size, 128), size)
            here = pl.ds(i * size, size)
            if back:
                o_ref[:, there] = x_ref[:, here]
            else:
                o_ref[:, here] = x_ref[:, there]


def reorder(arrays, back=False):
    at = lax.axis_index("fsdp").astype(jnp.int32).reshape(1)
    vmem = pl.BlockSpec(memory_space=pltpu.VMEM)
    return pl.pallas_call(
        functools.partial(reorder_kernel, back, len(arrays)),
        out_shape=[jax.ShapeDtypeStruct(a.shape, a.dtype) for a in arrays],
        in_specs=[pl.BlockSpec(memory_space=pltpu.SMEM)] + [vmem] * len(arrays),
        out_specs=[vmem] * len(arrays),
    )(at, *arrays)


def lay_kernel(plan, n, kv_of, rank_ref, *refs):
    blocks, outs = refs[:n], refs[n:]
    rank = rank_ref[0]
    for kind, src, size, out, base in plan:
        o_ref = outs[out]
        if kind == "slice":
            for k in range(n):
                owner = lax.rem(rank - k + n, n)
                there = pl.ds(pl.multiple_of(base + owner * size, 128), size)
                o_ref[:, there] = blocks[k][:, src : src + size].astype(F32)
        elif kind == "sum":
            total = blocks[0][:, src : src + size].astype(F32)
            for k in range(1, n):
                total += blocks[k][:, src : src + size].astype(F32)
            o_ref[:, base : base + size] = total
        elif kind == "kv":
            heads = o_ref.shape[1] // size
            pieces = [jnp.zeros((o_ref.shape[0], size), F32)] * heads
            for k in range(n):
                owner = lax.rem(rank - k + n, n)
                value = blocks[k][:, src : src + size].astype(F32)
                for h in range(heads):
                    pieces[h] = pieces[h] + jnp.where(kv_of(owner) == h, value, 0.0)
            o_ref[...] = jnp.concatenate(pieces, 1)
        else:
            value = [blocks[k][:, src : src + size].astype(F32) for k in range(n)]
            for p in range(n):
                total = jnp.zeros_like(value[0])
                for k in range(n):
                    owner = lax.rem(rank - k + n, n)
                    total = jnp.where(owner == p, value[k], total)
                o_ref[:, base + p * size : base + (p + 1) * size] = total


def lay(blocks, plan, widths, kv_of):
    n = len(blocks)
    rank = lax.axis_index("dp").astype(jnp.int32).reshape(1)
    vmem = pl.BlockSpec(memory_space=pltpu.VMEM)
    return pl.pallas_call(
        functools.partial(lay_kernel, plan, n, kv_of),
        out_shape=[jax.ShapeDtypeStruct((blocks[0].shape[0], w), F32) for w in widths],
        in_specs=[pl.BlockSpec(memory_space=pltpu.SMEM)] + [vmem] * n,
        out_specs=[vmem] * len(widths),
    )(rank, *blocks)


def peer_send(blocks):
    n = lax.axis_size("dp")
    return [blocks[0]] + [
        lax.ppermute(blocks[k], "dp", [(i, (i - k) % n) for i in range(n)])
        for k in range(n - 1, 0, -1)
    ]


def peer_scalar_sum(v):
    n = lax.axis_size("dp")
    total = v
    for m in range(1, n):
        got = lax.ppermute(v, "dp", [(i, (i - m) % n) for i in range(n)])
        total = total + jnp.roll(got, -m, 0)
    return total


def sum_level(values):
    while len(values) > 1:
        values = [values[i] + values[i + 1] for i in range(0, len(values), 2)]
    return values[0]


def sum_dp(v):
    n = lax.axis_size("dp")
    return [v] + [
        lax.ppermute(v, "dp", [(i, i ^ m) for i in range(n)]) for m in range(1, n)
    ]


def sum_fsdp(v, step=1, stop=None):
    n = stop or lax.axis_size("fsdp")
    while step < n:
        v = v + lax.ppermute(v, "fsdp", [(i, i ^ step) for i in range(lax.axis_size("fsdp"))])
        step *= 2
    return v


def transposed(m):
    return jnp.swapaxes(m, 0, 1)


def column(row):
    size = row.shape[1]
    return transposed(jnp.broadcast_to(row, (size, size)))


def columns(ref):
    return jnp.concatenate([column(ref[k])[:, :1] for k in range(ref.shape[0])], 0)


def exact(a, b, dims):
    return lax.dot_general(a, b, (dims, ((), ())), precision=HIGH, preferred_element_type=F32)


def quick(a, b, dims):
    return lax.dot_general(
        a.astype(BF), b.astype(BF), (dims, ((), ())), preferred_element_type=F32
    )


NN, NT, TN = ((1,), (0,)), ((1,), (1,)), ((0,), (0,))


def shift_down(x, lag):
    return jnp.concatenate([jnp.zeros((lag, x.shape[1]), x.dtype), x[: x.shape[0] - lag]], 0)


def shift_up(x, lag):
    return jnp.concatenate([x[lag:], jnp.zeros((lag, x.shape[1]), x.dtype)], 0)


def branch_common(start, proj, conv_p, head_p, sizes):
    rows, inner, both, _ = sizes
    t_col = lax.broadcasted_iota(jnp.int32, (rows, rows), 0)
    s_row = lax.broadcasted_iota(jnp.int32, (rows, rows), 1)
    start_t = start.astype(F32)
    keep = (start_t == transposed(start_t)) & (s_row <= t_col)
    first = start_t[:, :1].astype(jnp.int32)
    t_one = t_col[:, :1]
    conv_in = proj[:, inner : 2 * inner + both]
    conv = conv_in * conv_p[3:4]
    lagged = []
    for lag in range(1, 4):
        ok = t_one - lag >= first
        moved = jnp.where(ok, shift_down(conv_in, lag), 0.0)
        lagged.append((ok, moved))
        conv = conv + moved * conv_p[3 - lag : 4 - lag]
    pre = conv + conv_p[4:5]
    gate = jax.nn.sigmoid(pre)
    act = pre * gate
    x, b, c = act[:, :inner], act[:, inner : inner + both // 2], act[:, inner + both // 2 :]
    dt = proj[:, proj.shape[1] - 128 :] + head_p[2:3]
    delta = jnp.maximum(dt, 0.0) + jnp.log1p(jnp.exp(-jnp.abs(dt)))
    decay_log = -delta * jnp.exp(head_p[0:1])
    lower = (s_row <= t_col).astype(F32)
    cum = exact(lower, decay_log, NN)
    cum_t, delta_t = transposed(cum), transposed(delta)
    scores = exact(c, b, NT)

    def head_decay(h):
        gap = cum[:, h : h + 1] - cum_t[h : h + 1]
        return jnp.where(keep, jnp.exp(jnp.where(keep, gap, 0.0)), 0.0)

    return dict(
        t_col=t_col, s_row=s_row, keep=keep, first=first, t_one=t_one, conv_in=conv_in,
        lagged=lagged, pre=pre, gate=gate, x=x, b=b, c=c, dt=dt, delta=delta,
        decay_log=decay_log, lower=lower, delta_t=delta_t, scores=scores, head_decay=head_decay,
    )


def swap_halves(x):
    lane = lax.broadcasted_iota(jnp.int32, x.shape, 1)
    size, half = x.shape[1], HD // 2
    low = lane % HD < half
    return jnp.where(low, pltpu.roll(x, size - half, 1), pltpu.roll(x, half, 1))


def rotary(first, rows):
    lane = lax.broadcasted_iota(jnp.int32, (rows, 128), 1)
    t = lax.broadcasted_iota(jnp.int32, (rows, 128), 0)
    half = HD // 2
    frequency = jnp.exp((lane % half).astype(F32) * (-2.0 / HD * math.log(rope_base)))
    angle = (t - first).astype(F32) * frequency
    return jnp.cos(angle), jnp.where(lane % HD < half, -jnp.sin(angle), jnp.sin(angle))


def attn_common(q, kv, first, keep):
    rows = q.shape[0]
    lane = lax.broadcasted_iota(jnp.int32, (rows, 128), 1)
    low = lane < HD
    cosine, sine = rotary(first, rows)
    q_rot = q * cosine + swap_halves(q) * sine
    k_rot = kv * cosine + swap_halves(kv) * sine
    keys = jnp.where(low, k_rot, pltpu.roll(k_rot, HD, 1))
    values = jnp.where(low, pltpu.roll(kv, HD, 1), kv)
    probs, picks = [], []
    for h in range(2):
        pick = low if h == 0 else ~low
        logits = exact(jnp.where(pick, q_rot, 0.0), keys, NT) * HD ** (-0.5)
        logits = jnp.where(keep, logits, -1e30)
        expo = jnp.exp(logits - jnp.max(logits, -1, keepdims=True))
        probs.append(expo / jnp.sum(expo, -1, keepdims=True))
        picks.append(pick)
    return low, cosine, sine, q_rot, keys, values, probs, picks


def branch_forward(
    sizes, n, *refs
):
    a0_ref, a1_ref, g_ref, conv_ref, head_ref = refs[n : n + 5]
    normed_ref, proj_ref, y_ref, gated_ref, square_ref, x_ref = refs[n + 5 :]
    for k in range(n):

        @pl.when(pl.program_id(0) == k)
        def _():
            x_ref[...] = refs[k][...]

    rows, inner, _, heads = sizes
    width = g_ref.shape[1]
    x32 = x_ref[:, :width].astype(F32)
    scale = lax.rsqrt(jnp.mean(x32 * x32, -1, keepdims=True) + norm_eps)
    normed = (x32 * scale * g_ref[...]).astype(BF)
    normed_ref[...] = normed
    half = a0_ref.shape[0]
    proj = mm(normed[:, :half], a0_ref[...]) + mm(normed[:, half:], a1_ref[...])
    proj_ref[...] = proj
    start = x_ref[:, width:]
    conv_p, head_p = conv_ref[...], head_ref[...]
    v = branch_common(start, proj, conv_p, head_p, sizes)
    low = v["s_row"] < HD
    outs = []
    for pair in range(heads // 2):
        x_pair = v["x"][:, pair * 128 : pair * 128 + 128]
        y = []
        for h in (2 * pair, 2 * pair + 1):
            mixer = v["scores"] * v["head_decay"](h) * v["delta_t"][h : h + 1]
            y.append(quick(mixer, x_pair, NN))
        outs.append(jnp.where(low, y[0], y[1]))
    y = jnp.concatenate(outs, 1) + conv_p[5:6, :inner] * v["x"]
    z = proj[:, :inner]
    gated = y * (z * jax.nn.sigmoid(z))
    y_ref[...] = y
    gated_ref[...] = gated
    square = jnp.sum(gated * gated, -1, keepdims=True)
    square_ref[0] = transposed(jnp.broadcast_to(square, (rows, rows)))[:1]


def links(start):
    shape = start.shape
    t_col = lax.broadcasted_iota(jnp.int32, shape, 0)
    s_row = lax.broadcasted_iota(jnp.int32, shape, 1)
    return start[:, :1].astype(jnp.int32), (start == transposed(start)) & (s_row <= t_col)


def attn_forward(x_ref, qkv_ref, attn_ref, kept_ref):
    first, keep = links(x_ref[...].astype(F32))
    low, cosine, sine, q_rot, keys, values, probs, _ = attn_common(
        qkv_ref[:, :128], qkv_ref[:, 128:], first, keep
    )
    for i, value in enumerate((cosine, sine, q_rot, keys, values, *probs)):
        kept_ref[:, i * 128 : (i + 1) * 128] = value
    out = [quick(p, values, NN) for p in probs]
    attn_ref[...] = jnp.where(low, out[0], out[1]).astype(BF)


def branch_back_out(
    inner, low, n, *refs
):
    b0_ref, b1_ref, gated_ref, scale_ref, gm_ref = refs[n : n + 5]
    d_scaled_ref, d_attn_ref, inner_ref, g_gm_ref, dm_ref = refs[n + 5 :]
    dm = jnp.concatenate([r[...] for r in refs[:n]], 0)
    dm_ref[...] = dm
    d_mix = halved(dm, b0_ref[:, low:], b1_ref[:, low:])
    d_out = d_mix[:, :inner]
    gated = gated_ref[...]
    g_gm_ref[...] = jnp.sum(d_out * gated * columns(scale_ref), 0, keepdims=True)
    d_scaled = d_out * gm_ref[...]
    d_scaled_ref[...] = d_scaled
    dot = jnp.sum(d_scaled * gated, -1, keepdims=True)
    rows = inner_ref.shape[2]
    for k in range(inner_ref.shape[0]):
        block = jnp.broadcast_to(dot[k * rows : (k + 1) * rows], (rows, rows))
        inner_ref[k] = transposed(block)[:1]
    d_attn_ref[...] = d_mix[:, inner:]


def branch_back_attn(kept_ref, d_attn_ref, d_qkv_ref):
    rows = kept_ref.shape[0]
    kept = [kept_ref[:, i * 128 : (i + 1) * 128] for i in range(7)]
    cosine, sine, q_rot, keys, values, *probs = kept
    low = lax.broadcasted_iota(jnp.int32, (rows, 128), 1) < HD
    picks = [low, ~low]
    d_attn = d_attn_ref[...]
    d_q = []
    d_k = jnp.zeros((rows, 128), F32)
    d_v = jnp.zeros((rows, 128), F32)
    for p, pick in zip(probs, picks):
        d_head = jnp.where(pick, d_attn, 0.0)
        d_p = quick(d_head, values, NT)
        d_logit = p * (d_p - jnp.sum(d_p * p, -1, keepdims=True)) * HD ** (-0.5)
        d_q.append(quick(d_logit, keys, NN))
        d_k += quick(d_logit, jnp.where(pick, q_rot, 0.0), TN)
        d_v += quick(p, d_head, TN)
    d_q = jnp.where(low, d_q[0], d_q[1])
    d_k = d_k + pltpu.roll(d_k, HD, 1)
    d_v = d_v + pltpu.roll(d_v, HD, 1)
    d_q = d_q * cosine + swap_halves(d_q * sine)
    d_k = d_k * cosine + swap_halves(d_k * sine)
    d_qkv_ref[:, :128] = d_q.astype(BF)
    d_qkv_ref[:, 128:] = jnp.where(low, d_k, d_v).astype(BF)


def branch_back_mamba(
    sizes, q_at, x_ref, proj_ref, y_ref, gated_ref, d_scaled_ref, scale_ref, inner_ref,
    d_qkv_ref, conv_ref, head_ref, whole,
    d_proj_ref, g_conv_ref, g_head_ref, g_skip_ref,
):
    rows, inner, both, heads = sizes

    @pl.when(pl.program_id(0) == 0)
    def _():
        g_conv_ref[...] = jnp.zeros_like(g_conv_ref)
        g_head_ref[...] = jnp.zeros_like(g_head_ref)
        g_skip_ref[...] = jnp.zeros_like(g_skip_ref)

    proj = proj_ref[...]
    conv_p, head_p = conv_ref[...], head_ref[...]
    v = branch_common(x_ref[...], proj, conv_p, head_p, sizes)
    scale = column(scale_ref[0])[:, :1]
    dot = column(inner_ref[0])[:, :1]
    d_gated = scale * d_scaled_ref[...] - gated_ref[...] * (scale * scale * scale * dot / whole)
    z = proj[:, :inner]
    zs = jax.nn.sigmoid(z)
    d_y = d_gated * (z * zs)
    d_z = d_gated * y_ref[...] * (zs * (1.0 + z * (1.0 - zs)))
    d_proj_ref[:, :inner] = d_z.astype(BF)
    x, scores, delta_t = v["x"], v["scores"], v["delta_t"]
    g_skip_ref[...] += jnp.sum(d_y * x, 0, keepdims=True)
    low = v["s_row"] < HD
    d_x = []
    d_scores = jnp.zeros((rows, rows), F32)
    d_cum = jnp.zeros((rows, rows), F32)
    d_delta_rows, d_cum_rows = [], []
    for pair in range(heads // 2):
        at = slice(pair * 128, pair * 128 + 128)
        x_pair, dy_pair = x[:, at], d_y[:, at]
        parts = []
        for h in (2 * pair, 2 * pair + 1):
            pick = low if h % 2 == 0 else ~low
            decay = v["head_decay"](h)
            scored = scores * decay
            mixer = scored * delta_t[h : h + 1]
            d_mixer = quick(jnp.where(pick, dy_pair, 0.0), x_pair, NT)
            parts.append(quick(mixer, dy_pair, TN))
            d_scores += d_mixer * (decay * delta_t[h : h + 1])
            d_delta_rows.append(jnp.sum(d_mixer * scored, 0, keepdims=True))
            flow = d_mixer * mixer
            d_cum_rows.append(jnp.sum(flow, 0, keepdims=True))
            d_cum = jnp.where(v["s_row"] == h, jnp.sum(flow, -1, keepdims=True), d_cum)
        d_x.append(jnp.where(low, parts[0], parts[1]))
    blank = jnp.zeros((rows - heads, rows), F32)
    d_delta = transposed(jnp.concatenate(d_delta_rows + [blank], 0))
    d_cum = d_cum - transposed(jnp.concatenate(d_cum_rows + [blank], 0))
    d_log = exact(v["lower"], d_cum, TN)
    d_delta = d_delta - jnp.exp(head_p[0:1]) * d_log
    d_dt = d_delta * jax.nn.sigmoid(v["dt"])
    g_head_ref[0:1] += jnp.sum(d_log * v["decay_log"], 0, keepdims=True)
    g_head_ref[1:2] += jnp.sum(d_dt, 0, keepdims=True)
    d_proj_ref[:, d_proj_ref.shape[1] - 128 :] = d_dt.astype(BF)
    d_act = jnp.concatenate(
        d_x + [quick(d_scores, v["c"], TN), quick(d_scores, v["b"], NN)], 1
    )
    d_act = jnp.concatenate(
        [d_act[:, :inner] + conv_p[5:6, :inner] * d_y, d_act[:, inner:]], 1
    )
    gate = v["gate"]
    d_conv = d_act * (gate * (1.0 + v["pre"] * (1.0 - gate)))
    g_conv_ref[4:5] += jnp.sum(d_conv, 0, keepdims=True)
    g_conv_ref[3:4] += jnp.sum(d_conv * v["conv_in"], 0, keepdims=True)
    d_in = d_conv * conv_p[3:4]
    for lag, (ok, moved) in zip(range(1, 4), v["lagged"]):
        g_conv_ref[3 - lag : 4 - lag] += jnp.sum(d_conv * moved, 0, keepdims=True)
        back = shift_up(jnp.where(ok, d_conv, 0.0), lag)
        d_in = d_in + back * conv_p[3 - lag : 4 - lag]
    d_proj_ref[:, inner : 2 * inner + both] = d_in.astype(BF)
    d_proj_ref[:, q_at : q_at + 256] = d_qkv_ref[...]


def halved(left, w0, w1):
    half = w0.shape[0]
    return mm(left[:, :half], w0) + mm(left[:, half:], w1)


def put_rows(outs, left, w0, w1):
    value = jnp.concatenate([mul_t(left, w0), mul_t(left, w1)], 1)
    rows = left.shape[0] // len(outs)
    for k, o_ref in enumerate(outs):
        o_ref[...] = value[k * rows : (k + 1) * rows].astype(o_ref.dtype)
    return value


def rows_out(n, rows, width):
    return [out_of((rows, width), F32)] + [out_of((rows, width), BF)] * (n - 1)


def rows_kernel(low, high, left_ref, w0_ref, w1_ref, *outs):
    put_rows(outs, left_ref[...], w0_ref[:, low:high], w1_ref[:, low:high])


def back_in_kernel(width, span, left_ref, x_ref, w0_ref, w1_ref, g_in_ref, *outs):
    value = put_rows(outs, left_ref[...], w0_ref[:, :span], w1_ref[:, :span])
    x32 = x_ref[:, :width].astype(F32)
    scale = lax.rsqrt(jnp.mean(x32 * x32, -1, keepdims=True) + norm_eps)
    g_in_ref[...] = jnp.sum(value * x32 * scale, 0, keepdims=True)


def partial_rows(n, left, halves, low, high):
    rows, width = left.shape[0] // n, 2 * halves[0].shape[0]
    return pl.pallas_call(
        functools.partial(rows_kernel, low, high), out_shape=rows_out(n, rows, width)
    )(left, *halves)


def mix_kernel(low, gated_ref, scale_ref, gm_ref, attn_ref, w0_ref, w1_ref, mix_ref, *outs):
    scale = columns(scale_ref)
    mamba = (gated_ref[...] * scale * gm_ref[...]).astype(BF)
    mix = jnp.concatenate([mamba, attn_ref[...]], 1)
    mix_ref[...] = mix
    put_rows(outs, mix, w0_ref[:, low:], w1_ref[:, low:])


def ffn_kernel(size, n, *refs):
    cot_ref, w0_ref, w1_ref, act_ref, d_gu_ref, hid_ref, *outs = refs[n:]
    hid = jnp.concatenate([r[...] for r in refs[:n]], 0)
    hid_ref[...] = hid
    gu = halved(hid, w0_ref[:, : 2 * size], w1_ref[:, : 2 * size])
    gate, up = gu[:, :size], gu[:, size:]
    sig = jax.nn.sigmoid(gate)
    silu = gate * sig
    act_ref[...] = (silu * up).astype(BF)
    d_act = halved(cot_ref[...], w0_ref[:, 2 * size :], w1_ref[:, 2 * size :])
    d_gate = d_act * up * (sig * (1.0 + gate * (1.0 - sig)))
    d_gu = jnp.concatenate([d_gate.astype(BF), (d_act * silu).astype(BF)], 1)
    d_gu_ref[...] = d_gu
    put_rows(outs, d_gu, w0_ref[:, : 2 * size], w1_ref[:, : 2 * size])


def row_spec(*shape):
    return pl.BlockSpec(shape, lambda i: (i,) + (0,) * (len(shape) - 1))


def fixed_spec(a):
    return pl.BlockSpec(a.shape, lambda i: (0,) * len(a.shape))


def out_of(shape, dtype):
    return jax.ShapeDtypeStruct(shape, dtype)


def rms_scale(x):
    return lax.rsqrt(jnp.mean(x * x, -1, keepdims=True) + norm_eps)


def rms_back(x, scale, gain, d_out):
    scaled = d_out * gain
    inner = jnp.mean(scaled * x, -1, keepdims=True)
    return scale * scaled - x * (scale * scale * scale * inner), jnp.sum(d_out * x * scale, 0)


def body(
    tokens,
    segment_ids,
    cotangent,
    w_in,
    w_q,
    w_k,
    w_v,
    w_o,
    w_out,
    w_gate,
    w_up,
    w_down,
    g_in,
    g_ff,
    g_mamba,
    conv_weight,
    conv_bias,
    a_log,
    d_skip,
    dt_bias,
):
    n = lax.axis_size("dp")
    rank = lax.axis_index("dp")
    rows, width = tokens.shape
    inner, channels, heads = g_mamba.shape[0], conv_bias.shape[0], a_log.shape[0]
    hidden = w_gate.shape[1]
    q_heads, kv_heads = w_q.shape[1] // HD, w_k.shape[1] // HD
    my_inner, my_heads, my_hidden, my_q = inner // n, heads // n, hidden // n, q_heads // n
    per_kv = q_heads // kv_heads
    assert heads % n == 0 and q_heads % n == 0 and hidden % n == 0 and per_kv % my_q == 0
    both = channels - inner
    qc = my_q * HD

    cube = is_cube(width)
    tail_pad = -my_heads % 128
    assert rows <= 256
    start = (segment_ids - segment_ids[0]).astype(BF)
    start = jnp.broadcast_to(start[:, None], (rows, 128))
    o = 2 * my_inner + both
    span = o + qc + 2 * HD + my_heads + tail_pad
    mc = my_inner + qc
    vmem = pl.BlockSpec(memory_space=pltpu.VMEM)
    shards = (w_in.T, w_q, w_k, w_v, w_o, w_out, w_gate, w_up, w_down)
    dims = (inner, channels, my_inner, my_heads, my_hidden, qc, my_q, per_kv, n)
    sh_a, sh_b = pl.pallas_call(
        functools.partial(slice_kernel, dims),
        out_shape=[
            out_of((w_in.shape[0], span + mc), BF),
            out_of((w_in.shape[0], 3 * my_hidden), BF),
        ],
        in_specs=[pl.BlockSpec(memory_space=pltpu.SMEM)] + [vmem] * 9,
        out_specs=[vmem] * 2,
    )(rank.astype(jnp.int32).reshape(1), *shards)
    if cube:
        parts_a = gather_start(sh_a)
        tokens, cotangent, g_in, g_ff = reorder(
            [tokens, cotangent, g_in.reshape(1, width), g_ff.reshape(1, width)]
        )
    first = peer_blocks(jnp.concatenate([tokens, start], 1))
    if cube:
        parts_a, tok_held = tie((parts_a, first[-2]))
        own_a = jnp.concatenate(parts_a, 0)
        halves_a = [own_a, flip(own_a, 1)]
        tok_blocks = first
    else:
        tok_held = first[-2]
        tok_blocks = first
        full_a = lax.all_gather(sh_a, "fsdp", axis=0, tiled=True)
        halves_a = [full_a[: width // 2], full_a[width // 2 :]]

    if cube:
        sh_b, parts_a = tie((sh_b, parts_a))
        parts_b = gather_start(sh_b)
    cot_first, _ = tie((cotangent, tok_held))
    cot_blocks = peer_direct(cot_first)

    assert n == 4 and lax.axis_size("fsdp") & (lax.axis_size("fsdp") - 1) == 0
    assert rows == 128 and qc == 128 and 2 * HD == 128 and conv_weight.shape[0] == 4
    assert my_heads % 2 == 0 and both % 256 == 0 and inner // heads == HD
    assert o % 256 == 0 and width % 128 == 0
    cw = jnp.concatenate(
        [cols(conv_weight, rank * my_inner, my_inner), conv_weight[:, inner:]], 1
    )
    cb = jnp.concatenate(
        [lax.dynamic_slice(conv_bias, (rank * my_inner,), (my_inner,)), conv_bias[inner:]]
    )

    def mine(p, size):
        return lax.dynamic_slice(p, (rank * size,), (size,))

    gm = mine(g_mamba, my_inner)

    sizes = (rows, my_inner, both, my_heads)
    skip = jnp.repeat(mine(d_skip, my_heads), HD)
    conv_p = jnp.concatenate(
        [cw, cb[None], jnp.pad(skip, (0, both))[None], jnp.zeros((2, cw.shape[1]), F32)], 0
    )
    head_p = jnp.stack(
        [mine(a_log, my_heads), mine(d_skip, my_heads), mine(dt_bias, my_heads)], 0
    )
    head_p = jnp.pad(head_p, ((0, 5), (0, 128 - my_heads)))
    gm = gm.reshape(1, my_inner)
    g_in_row = g_in.reshape(1, width)
    count = n * rows
    normed, proj, y, gated, square, first = pl.pallas_call(
        functools.partial(branch_forward, sizes, n),
        grid=(n,),
        in_specs=[fixed_spec(a) for a in tok_blocks]
        + [pl.BlockSpec((a.shape[0], span), lambda i: (0, 0)) for a in halves_a]
        + [fixed_spec(a) for a in (g_in_row, conv_p, head_p)],
        out_specs=[
            row_spec(rows, width),
            row_spec(rows, span),
            row_spec(rows, my_inner),
            row_spec(rows, my_inner),
            row_spec(1, 1, rows),
            row_spec(rows, width + 128),
        ],
        out_shape=[
            out_of((count, width), BF),
            out_of((count, span), F32),
            out_of((count, my_inner), F32),
            out_of((count, my_inner), F32),
            out_of((n, 1, rows), F32),
            out_of((count, width + 128), BF),
        ],
    )(*tok_blocks, *halves_a, g_in_row, conv_p, head_p)
    square = peer_scalar_sum(square.reshape(n, rows))
    start_spec = pl.BlockSpec((rows, 128), lambda i: (i, width // 128))
    qkv_spec = pl.BlockSpec((rows, 256), lambda i: (i, o // 256))
    attn, kept = pl.pallas_call(
        attn_forward,
        grid=(n,),
        in_specs=[start_spec, qkv_spec],
        out_specs=[row_spec(rows, qc), row_spec(rows, 7 * 128)],
        out_shape=[out_of((count, qc), BF), out_of((count, 7 * 128), F32)],
    )(first, proj)
    scale_rows = lax.rsqrt(square / inner + norm_eps).reshape(n, 1, rows)
    shapes = rows_out(n, rows, width)
    mix_in, *mix_parts = pl.pallas_call(
        functools.partial(mix_kernel, span),
        out_shape=[out_of((count, mc), BF)] + shapes,
    )(gated, scale_rows, gm, attn, *halves_a)
    mix_parts = peer_send(mix_parts)
    if cube:
        mix_parts, cot_blocks = tie((mix_parts, cot_blocks))
        own_b = jnp.concatenate(parts_b, 0)
        halves_b = [own_b, flip(own_b, 1)]
    else:
        full_b = lax.all_gather(sh_b, "fsdp", axis=0, tiled=True)
        halves_b = [full_b[: width // 2], full_b[width // 2 :]]
    cot_all = jnp.concatenate(cot_blocks, 0)
    tok32 = tokens.astype(F32)
    mixed = tok32 + add_up(mix_parts)
    f_scale = rms_scale(mixed)
    hid_blocks = peer_blocks((mixed * f_scale * g_ff).astype(BF))
    act, d_gu, hid_all, *d_hidden = pl.pallas_call(
        functools.partial(ffn_kernel, my_hidden, n),
        out_shape=[out_of((count, my_hidden), BF), out_of((count, 2 * my_hidden), BF)]
        + [out_of((count, width), BF)]
        + shapes,
    )(*hid_blocks, cot_all, *halves_b)
    d_hidden = peer_send(d_hidden)
    c_pairs = [(hid_all, d_gu), (cot_all, act)]
    if cube:
        c_own = scatter_own(c_pairs, scatter_first(c_pairs))
        grad_c = scatter_rest(c_own)
        d_hidden, c_own = tie((d_hidden, c_own))
    else:
        grad_c = grads(c_pairs, 0, width)
    d_mixed_n, grad_g_ff = rms_back(mixed, f_scale, g_ff, add_up(d_hidden))
    d_mixed = cotangent.astype(F32) + d_mixed_n
    dm_blocks = peer_blocks(d_mixed.astype(BF))
    if cube:
        grad_c = add_up(grad_c).astype(BF)
    else:
        grad_c = lax.psum_scatter(grad_c, "fsdp", scatter_dimension=0, tiled=True)
    c_blocks = [grad_c]
    for _ in range(1, n):
        c_blocks.append(next_peer(c_blocks[-1]))
    out_parts = partial_rows(n, act, halves_b, 2 * my_hidden, 3 * my_hidden)
    out_parts = peer_send(out_parts)
    d_scaled, d_attn, m_inner, grad_gm, dm_all = pl.pallas_call(
        functools.partial(branch_back_out, my_inner, span, n),
        out_shape=[
            out_of((count, my_inner), F32),
            out_of((count, qc), F32),
            out_of((n, 1, rows), F32),
            out_of((1, my_inner), F32),
            out_of((count, width), BF),
        ],
    )(*dm_blocks, *halves_a, gated, scale_rows, gm)
    d_qkv = pl.pallas_call(
        branch_back_attn,
        grid=(n,),
        in_specs=[row_spec(rows, 7 * 128), row_spec(rows, qc)],
        out_specs=row_spec(rows, 256),
        out_shape=out_of((count, 256), BF),
        cost_estimate=pl.CostEstimate(
            flops=30 * count * rows * 128, bytes_accessed=count * 5000, transcendentals=count * 512
        ),
    )(kept, d_attn)
    m_inner = peer_scalar_sum(m_inner.reshape(n, rows)).reshape(n, 1, rows)
    m_inner, d_qkv = tie((m_inner, d_qkv))
    d_proj, g_conv, g_head, g_skip = pl.pallas_call(
        lambda *refs: branch_back_mamba(sizes, o, *refs[:10], float(inner), *refs[10:]),
        grid=(n,),
        in_specs=[
            start_spec,
            row_spec(rows, span),
            row_spec(rows, my_inner),
            row_spec(rows, my_inner),
            row_spec(rows, my_inner),
            row_spec(1, 1, rows),
            row_spec(1, 1, rows),
            row_spec(rows, 256),
            fixed_spec(conv_p),
            fixed_spec(head_p),
        ],
        out_specs=[
            row_spec(rows, span),
            fixed_spec(conv_p),
            fixed_spec(head_p),
            fixed_spec(gm),
        ],
        out_shape=[
            out_of((count, span), BF),
            out_of(conv_p.shape, F32),
            out_of(head_p.shape, F32),
            out_of((1, my_inner), F32),
        ],
    )(first, proj, y, gated, d_scaled, scale_rows, m_inner, d_qkv, conv_p, head_p)
    a_pairs = [(dm_all, mix_in), (normed, d_proj)]
    if cube:
        got = scatter_first(a_pairs)
        d_proj, _ = tie((d_proj, a_pairs))
    grad_g_in, *d_normed = pl.pallas_call(
        functools.partial(back_in_kernel, width, span),
        out_shape=[out_of((1, width), F32)] + shapes,
    )(d_proj, first, *halves_a)

    def place(v):
        spot = (jnp.arange(n) == rank).astype(F32)
        spread = spot[:, None, None] * v.reshape(v.shape[:-1] + (1, -1, 128))
        return spread.reshape(-1, 128)

    def ordered(v):
        v = v.reshape(-1, 128)
        if not cube:
            return v
        block = jnp.array(ORDER) ^ lax.axis_index("fsdp")
        hit = (jnp.arange(8)[:, None] == block[None, :]).astype(F32)
        v = v.reshape(8, 1, -1)
        return jnp.sum(hit.T[:, :, None] * v, 0).reshape(-1, 128)

    def head_row(v):
        spot = (jnp.arange(n) == rank).astype(F32)
        return jnp.pad((spot[:, None] * v[None]).reshape(1, -1), ((0, 0), (0, 128 - heads)))

    grad_gm, g_cw, g_cb = grad_gm[0], g_conv[:4], g_conv[4]
    g_al, g_db = g_head[0, :my_heads], g_head[1, :my_heads]
    g_ds = jnp.sum(g_skip.reshape(my_heads, HD), 1)
    small = [ordered(grad_g_in), ordered(grad_g_ff), place(grad_gm)]
    for row in range(g_cw.shape[0]):
        small += [place(g_cw[row, :my_inner]), g_cw[row, my_inner:].reshape(-1, 128)]
    small += [place(g_cb[:my_inner]), g_cb[my_inner:].reshape(-1, 128)]
    small += [head_row(g_al), head_row(g_ds), head_row(g_db)]
    flat = jnp.concatenate(small)
    flat = jnp.pad(flat, ((0, -flat.shape[0] % 8), (0, 0)))
    flat = sum_dp(flat)

    if cube:
        own = scatter_own(a_pairs, got)
        grad_a = scatter_rest(own)
        d_normed, c_blocks, out_parts, own = tie((d_normed, c_blocks, out_parts, own))
        d_normed = peer_send(d_normed)
        grad_a = add_up(grad_a).astype(BF)
    else:
        d_normed = peer_send(d_normed)
        grad_a = lax.psum_scatter(
            grads(a_pairs, 0, width), "fsdp", scatter_dimension=0, tiled=True
        )
    output = (mixed + add_up(out_parts)).astype(BF)
    a_blocks = [grad_a, next_peer(grad_a)]
    while len(a_blocks) < n:
        a_blocks[-1], flat = tie((a_blocks[-1], flat))
        a_blocks.append(next_peer(a_blocks[-1]))
        if len(a_blocks) == 3:
            flat = sum_fsdp(sum_level(flat), 1, 4)
    flat = sum_fsdp(flat, 4)
    a_blocks[2], d_normed = tie((a_blocks[2], d_normed))
    d_tok_n, _ = rms_back(tok32, rms_scale(tok32), g_in, add_up(d_normed))
    grad_tokens = (d_mixed + d_tok_n).astype(BF)
    if cube:
        output, grad_tokens = reorder([output, grad_tokens], True)


    def kv_of(owner):
        return owner * my_q // per_kv

    grad_gate, grad_up, grad_down = lay(
        c_blocks, [("slice", i * my_hidden, my_hidden, i, 0) for i in range(3)], [hidden] * 3, kv_of
    )
    grad_in, grad_q, grad_k, grad_v, grad_out, grad_o = lay(
        a_blocks,
        [
            ("slice", 0, my_inner, 4, 0),
            ("slice", my_inner, qc, 5, 0),
            ("slice", mc, my_inner, 0, 0),
            ("slice", mc + my_inner, my_inner, 0, inner),
            ("sum", mc + 2 * my_inner, both, 0, 2 * inner),
            ("slice", mc + o, qc, 1, 0),
            ("kv", mc + o + qc, HD, 2, 0),
            ("kv", mc + o + qc + HD, HD, 3, 0),
            ("tail", mc + o + qc + 2 * HD, my_heads, 0, inner + channels),
        ],
        [w_in.shape[1], w_q.shape[1], w_k.shape[1], w_v.shape[1], inner, w_o.shape[1]],
        kv_of,
    )

    sizes = [width, width, inner, g_cw.shape[0] * channels, channels]
    sums, at = [], 0
    for size in sizes:
        sums.append(flat[at : at + size // 128].reshape(-1))
        at += size // 128
    for i in range(3):
        sums.append(flat[at + i, :heads])
    return (
        output,
        grad_tokens,
        grad_in,
        grad_q,
        grad_k,
        grad_v,
        grad_o,
        grad_out,
        grad_gate,
        grad_up,
        grad_down,
        sums[0],
        sums[1],
        sums[2],
        sums[3].reshape(conv_weight.shape),
        sums[4],
        sums[5],
        sums[6],
        sums[7],
    )


def solution(mesh):
    rows, shard, whole = P(("fsdp", "dp"), None), P("fsdp", None), P()
    in_specs = (rows, P(("fsdp", "dp")), rows) + (shard,) * 9 + (whole,) * 8
    out_specs = (rows, rows) + (shard,) * 9 + (whole,) * 8

    return jax.shard_map(body, mesh=mesh, in_specs=in_specs, out_specs=out_specs, check_vma=False)
```
